32 devices in a mesh: row: 4 (over y, x), col: 8 (over z, core).
Axes of the slice: x: 2, y: 2, z: 4, core: 2. Of those that a mesh axis runs over, the one named last changes fastest.
Arguments:
- left_blocks: float32 [4, 8, 42, 128, 128], P('row', 'col'), may hold values from -1 to 1
- right_blocks: float32 [4, 8, 42, 128, 128], P('row', 'col'), may hold values from -1 to 1
- left_send: int32 [4, 8, 8, 8], P('row', 'col'), may hold values from -1 to 41, as said below
- left_place: int32 [4, 8, 2, 32], P('row', 'col'), may hold values from -1 to 63, as said below
- right_send: int32 [4, 8, 4, 16], P('row', 'col'), may hold values from -1 to 41, as said below
- right_place: int32 [4, 8, 2, 32], P('row', 'col'), may hold values from -1 to 63, as said below
- triples: int32 [4, 8, 2, 2, 3, 384], P('row', 'col'), may hold values from -1 to 31, as said below
Outputs:
- product_blocks: float32 [4, 8, 42, 128, 128], P('row', 'col')
The draws below stay inside these ranges and needn't reach their ends.
Inputs may be any that keep to these rules, and one draw needn't show every extreme that they name: `left_send`: each owner's 42 local blocks are each named exactly once over all peers and bucket slots; the other slots are -1. In every grid row one device receives a full bucket of 8 blocks from every owner. `left_place`: every received live position is named exactly once over a device's two panels, and no empty position is named. `right_send`: each owner's 42 local blocks are each named exactly once over all peers and bucket slots; the other slots are -1. In every grid column one device receives a full bucket of 16 blocks from every owner. `right_place`: every received live position is named exactly once over a device's two panels, and no empty position is named. For each image and stop the live triples come first and the rest are -1 in all three entries; some image and stop has 384 live triples.
All inputs are finite; a program needn't handle non-finite values.
Results may differ from the reference program's by a relative error of at most 0.0003.
Values sent between devices are 32-bit elements; how exact they have to be, the bound alone decides.
No kernel may reach another device: no remote copies, remote signals or barrier semaphores. Data moves between devices by JAX's collectives and lax.ppermute only.
A program may use at most 128 MiB of HBM per device.

```python
import jax
import jax.numpy as jnp
from jax import lax

BS = 128
PANEL = 32
PAIRS = 384
GRID_R = 4
GRID_C = 8
OWN = 42
SEND_A = 8
SEND_B = 16


def route_tables(key, groups, peer_count, per_peer, owned, panel_slots):
    slot_count = peer_count * per_peer

    def group_tables(group_key):
        full_key, rest_key = jax.random.split(group_key)
        full_peer = jax.random.randint(full_key, (), 0, peer_count)
        key_list = jax.random.split(rest_key, peer_count + 1)

        def sender_list(sender_key):
            first_key, second_key = jax.random.split(sender_key)
            scores = jax.random.permutation(first_key, slot_count).astype(jnp.int32)
            bucket_owner = jnp.arange(slot_count, dtype=jnp.int32) // per_peer
            within = jnp.arange(slot_count, dtype=jnp.int32) % per_peer
            scores = jnp.where(bucket_owner == full_peer, within - per_peer, scores)
            ranking = jnp.argsort(jnp.argsort(scores)).astype(jnp.int32)
            labels = jax.random.permutation(second_key, owned).astype(jnp.int32)
            return jnp.where(ranking < owned, labels[jnp.clip(ranking, 0, owned - 1)], -1).astype(jnp.int32)
        send_table = jax.vmap(sender_list)(key_list[:peer_count]).reshape(peer_count, peer_count, per_peer)
        present = send_table >= 0
        present_recv = jnp.transpose(present, (1, 0, 2)).reshape(peer_count, slot_count)
        place_keys = jax.random.split(key_list[peer_count], peer_count)

        def receiver_list(receiver_key, alive):
            shuffled = jax.random.permutation(receiver_key, slot_count).astype(jnp.int32)
            return jnp.where(alive[shuffled], shuffled, -1).astype(jnp.int32)
        place_table = jax.vmap(receiver_list)(place_keys, present_recv)
        return (send_table, place_table.reshape(peer_count, 2, panel_slots))
    return jax.vmap(group_tables)(jax.random.split(key, groups))


def left_tables(key):
    return route_tables(jax.random.fold_in(key, 11), GRID_R, GRID_C, SEND_A, OWN, PANEL)


def right_tables(key):
    send_table, place_table = route_tables(jax.random.fold_in(key, 23), GRID_C, GRID_R, SEND_B, OWN, PANEL)
    return (jnp.transpose(send_table, (1, 0, 2, 3)), jnp.transpose(place_table, (1, 0, 2, 3)))


def draw_left_send(key, part):
    return left_tables(key)[0]


def draw_left_place(key, part):
    return left_tables(key)[1]


def draw_right_send(key, part):
    return right_tables(key)[0]


def draw_right_place(key, part):
    return right_tables(key)[1]


def draw_triples(key, part):
    first_key, second_key, third_key = jax.random.split(key, 3)
    shape = (GRID_R, GRID_C, 2, 2)
    counts = jax.random.randint(first_key, shape, PAIRS // 2, PAIRS + 1)
    busiest = jax.random.randint(second_key, (), 0, GRID_R * GRID_C * 4)
    counts = jnp.where(jnp.arange(GRID_R * GRID_C * 4, dtype=jnp.int32).reshape(shape) == busiest, PAIRS, counts)
    index = jax.random.randint(third_key, shape + (3, PAIRS), 0, PANEL)
    present = jnp.arange(PAIRS, dtype=jnp.int32) < counts[..., None, None]
    return jnp.where(present, index, -1).astype(jnp.int32)


def shard_levels(rng, dims, cuts, smallest, high):
    level, own = 1.0, jax.random.fold_in(rng, 6)
    for axis_at, parts in cuts:
        draws = jnp.exp(jax.random.uniform(jax.random.fold_in(own, axis_at), (parts,), jnp.float32, smallest / len(cuts), high / len(cuts)))
        level = level * jnp.repeat(draws, dims[axis_at] // parts).reshape([-1 if axis == axis_at else 1 for axis in range(len(dims))])
    return level


def bell_draw(key, shape, deviation, bound, cuts=(), kind=jnp.bfloat16):
    entries = jax.random.normal(key, shape, jnp.float32) * deviation
    if len(cuts) > 0:
        entries = shard_levels(key, shape, cuts, -0.22, 0.18) * entries
    return jnp.clip(entries, min=-bound, max=bound).astype(kind)


def setup_inputs(seed: int = 0) -> dict:
    keys = jax.random.split(jax.random.key(seed), 8)
    return {
        "left_blocks": bell_draw(keys[0], (GRID_R, GRID_C, OWN, BS, BS), (BS // 4) ** -0.5, 1.0, ((0, 4), (1, 8)), jnp.float32),
        "right_blocks": bell_draw(keys[1], (GRID_R, GRID_C, OWN, BS, BS), (BS // 4) ** -0.5, 1.0, ((0, 4), (1, 8)), jnp.float32),
        "left_send": draw_left_send(jax.random.fold_in(keys[7], 71), 0),
        "left_place": draw_left_place(jax.random.fold_in(keys[7], 71), 0),
        "right_send": draw_right_send(jax.random.fold_in(keys[7], 71), 0),
        "right_place": draw_right_place(jax.random.fold_in(keys[7], 71), 0),
        "triples": draw_triples(jax.random.fold_in(keys[7], 71), 0),
    }


def deliver(owned, send_table, place_table):
    peer_count = send_table.shape[1]
    per_peer = send_table.shape[2]
    present = place_table >= 0
    position = jnp.where(present, place_table, 0)
    source = position // per_peer
    within = position % per_peer
    receiver = jnp.arange(peer_count, dtype=jnp.int32).reshape(peer_count, 1, 1)
    local_index = send_table[source, receiver, within]
    usable = present & (local_index >= 0)
    blocks = owned[source, jnp.where(usable, local_index, 0)]
    return jnp.where(usable[..., None, None], blocks, jnp.zeros((), owned.dtype))


def give_back(panels, send_table, place_table):
    peer_count = send_table.shape[1]
    per_peer = send_table.shape[2]
    present = place_table >= 0
    position = jnp.where(present, place_table, 0)
    source = position // per_peer
    within = position % per_peer
    receiver = jnp.arange(peer_count, dtype=jnp.int32).reshape(peer_count, 1, 1)
    local_index = send_table[source, receiver, within]
    usable = present & (local_index >= 0)
    target = jnp.where(usable, source * OWN + local_index, peer_count * OWN).astype(jnp.int32)
    tail = panels.shape[-2:]
    flattened = jnp.zeros((peer_count * OWN,) + tail, panels.dtype)
    flattened = flattened.at[target.reshape(-1)].set(panels.reshape((-1,) + tail), mode="drop")
    return flattened.reshape((peer_count, OWN) + tail)


def image_order(array):
    moved = jnp.moveaxis(array, 2, 0)
    return moved.reshape((moved.shape[0] * moved.shape[1],) + moved.shape[2:])


def device_order(array):
    split = array.reshape((2, array.shape[0] // 2) + array.shape[1:])
    return jnp.moveaxis(split, 0, 2)


def multiply(left_panel, right_panel, lists):
    present = lists[0] >= 0
    left_pick = left_panel[jnp.where(present, lists[0], 0)]
    right_pick = right_panel[jnp.where(present, lists[1], 0)]
    product = jnp.einsum("pik,pkj->pij", left_pick, right_pick, precision=lax.Precision.HIGHEST)
    product = jnp.where(present[:, None, None], product, jnp.zeros((), product.dtype))
    return jax.ops.segment_sum(product, jnp.where(present, lists[2], 0), num_segments=left_panel.shape[0])


def reference(left_blocks, right_blocks, left_send, left_place, right_send, right_place, triples):
    left_first = jax.vmap(deliver)(left_blocks, left_send, left_place)
    right_first = jax.vmap(deliver, in_axes=1, out_axes=1)(right_blocks, right_send, right_place)
    left_zero = image_order(left_first)
    right_zero = image_order(right_first)
    left_one = jnp.roll(left_zero, -1, axis=1)
    right_one = jnp.roll(right_zero, -1, axis=0)
    lists = image_order(triples)
    image_count = left_zero.shape[0] * left_zero.shape[1]

    def flatten(array):
        return array.reshape((image_count,) + array.shape[2:])

    def per_image(record):
        left_a, right_a, left_b, right_b, image_lists = record
        return multiply(left_a, right_a, image_lists[0]) + multiply(left_b, right_b, image_lists[1])

    products = lax.map(per_image, (flatten(left_zero), flatten(right_zero), flatten(left_one), flatten(right_one), flatten(lists)))
    product_panel = device_order(products.reshape(left_zero.shape))
    return jax.vmap(give_back)(product_panel, left_send, left_place)
```

```python
import functools

import jax
import jax.numpy as jnp
from jax import lax
from jax.experimental import pallas as pl
from jax.experimental.pallas import tpu as pltpu
from jax.sharding import PartitionSpec as P

GROUP = 4
SHIFT = 1024


def shifted(value, axis, steps):
    count = lax.axis_size(axis)
    pairs = [(source, (source + steps) % count) for source in range(count)]
    return lax.ppermute(value, axis, pairs)


def swapped(value, axis, mask):
    count = lax.axis_size(axis)
    return lax.ppermute(value, axis, [(source, source ^ mask) for source in range(count)])


def spread(piece, axis, masks):
    held = {0: piece}
    for mask in masks:
        held.update({mask ^ key: swapped(value, axis, mask) for key, value in list(held.items())})
    return held


def plan_body(sizes, place_ref, triple_ref, left_ref, left_next_ref, table_ref, code_ref, slot_ref, bound_ref,
              left_at, right_at, out_at, raw_code, raw_key, count_ref):
    rows, cols, own, per_left, per_right, panel, pairs = sizes
    row = place_ref[0]
    half = per_left // 2
    slots = cols * per_left
    zero_code = 2 * slots * SHIFT

    def tables(index, _):
        stop = index // (2 * panel)
        image = (index // panel) % 2
        slot = index % panel
        here = left_ref[image, slot]
        there = left_next_ref[image, slot]
        left = jnp.where(stop == 0, here, there)
        left_at[index] = jnp.where(left >= 0, stop * slots + left, -1)
        target = lax.rem(row + stop, rows)
        turned = jnp.where((stop == 1) & (row == rows - 1), 1 - image, image)
        place = table_ref[target ^ row, rows * per_right + turned * panel + slot]
        safe = jnp.maximum(place, 0)
        source = (safe // per_right) ^ row
        block = table_ref[source, target * per_right + safe % per_right]
        right_at[index] = jnp.where((place >= 0) & (block >= 0), source * own + block, -1)
        owner = jnp.maximum(here, 0) // per_left
        within = jnp.maximum(here, 0) % per_left
        spot = (within // half) * (cols * half) + owner * half + within % half
        out_at[image * panel + slot] = jnp.where(here >= 0, spot, -1)
        return 0

    lax.fori_loop(0, 4 * panel, tables, 0)

    def clear(index, _):
        count_ref[index] = 0
        return 0

    lax.fori_loop(0, slots + 1, clear, 0)
    total = jnp.int32(0)
    for image in range(2):
        for stop in range(2):
            base = (stop * 2 + image) * panel

            def read(index, found):
                a = triple_ref[image, stop, 0, index]
                b = triple_ref[image, stop, 1, index]
                t = triple_ref[image, stop, 2, index]
                left = left_at[base + jnp.maximum(a, 0)]
                right = right_at[base + jnp.maximum(b, 0)]
                spot = out_at[image * panel + jnp.maximum(t, 0)]
                live = (a >= 0) & (left >= 0) & (right >= 0) & (spot >= 0)
                raw_code[found] = left * SHIFT + right
                raw_key[found] = spot
                key = jnp.where(live, spot, slots)
                count_ref[key] = count_ref[key] + 1
                return found + live.astype(jnp.int32)

            total = lax.fori_loop(0, pairs, read, total)

    def fill(index, _):
        code_ref[index] = zero_code
        return 0

    lax.fori_loop(0, code_ref.shape[0], fill, 0, unroll=8)

    bound_ref[0] = 0
    done = jnp.int32(0)
    for part in range(2):

        def prefix(key, group):
            groups = (count_ref[key] + GROUP - 1) // GROUP

            def label(index, _):
                slot_ref[index] = key
                return 0

            lax.fori_loop(group, group + groups, label, 0)
            count_ref[key] = group * GROUP
            return group + groups

        done = lax.fori_loop(part * (slots // 2), (part + 1) * (slots // 2), prefix, done)
        bound_ref[part + 1] = done

    def place(index, _):
        key = raw_key[index]
        spot = count_ref[key]
        code_ref[spot] = raw_code[index]
        count_ref[key] = spot + 1
        return 0

    lax.fori_loop(0, total, place, 0)


def make_plan(row, triples, left_place, left_next, table, sizes):
    rows, cols, own, per_left, per_right, panel, pairs = sizes
    slots = cols * per_left
    room = 4 * pairs + slots * GROUP
    smem = pl.BlockSpec(memory_space=pltpu.SMEM)
    return pl.pallas_call(
        functools.partial(plan_body, sizes),
        out_shape=(
            jax.ShapeDtypeStruct((room,), jnp.int32),
            jax.ShapeDtypeStruct((room // GROUP,), jnp.int32),
            jax.ShapeDtypeStruct((4,), jnp.int32),
        ),
        in_specs=[smem] * 5,
        out_specs=(smem, smem, smem),
        scratch_shapes=[
            pltpu.SMEM((4 * panel,), jnp.int32),
            pltpu.SMEM((4 * panel,), jnp.int32),
            pltpu.SMEM((2 * panel,), jnp.int32),
            pltpu.SMEM((4 * pairs + 8,), jnp.int32),
            pltpu.SMEM((4 * pairs + 8,), jnp.int32),
            pltpu.SMEM((slots + 1,), jnp.int32),
        ],
        name="plan",
    )(row, triples, left_place, left_next, table)


CHUNK = 8


def compute_body(spans, slots, own, code_ref, slot_ref, bound_ref, *rest):
    sources = rest[: len(spans)]
    out_ref = rest[len(spans)]
    lefts, rights, total, raw, sems, out_sem = rest[len(spans) + 1 :]
    size = raw.shape[-1]
    steps = []
    for source, (side, base) in zip(sources, spans):
        count = source.shape[0]
        for start in range(0, count, CHUNK):
            steps.append((source, start, min(CHUNK, count - start), side, base + start))

    def copy(step):
        source, start, count, _, _ = steps[step]
        slot = step % 2
        return pltpu.make_async_copy(
            source.at[pl.ds(start, count)], raw.at[slot, pl.ds(0, count)], sems.at[slot]
        )

    copy(0).start()
    copy(1).start()
    total[...] = jnp.zeros_like(total)
    lefts[2 * slots] = jnp.zeros(lefts.shape[1:], lefts.dtype)
    for step in range(len(steps)):
        copy(step).wait()
        _, _, count, side, base = steps[step]
        target = lefts if side == 0 else rights

        def convert(index, _, slot=step % 2, target=target, base=base):
            value = raw[slot, index]
            high = value.astype(jnp.bfloat16)
            low = (value - high.astype(jnp.float32)).astype(jnp.bfloat16)
            target[base + index, :, 0:size] = high
            target[base + index, :, size : 2 * size] = low
            return 0

        lax.fori_loop(0, count, convert, 0)
        if step + 2 < len(steps):
            copy(step + 2).start()

    def multiply(group, _):
        spot = slot_ref[group]
        parts_left, parts_right = [], []
        for index in range(GROUP):
            code = code_ref[group * GROUP + index]
            parts_left.append(lefts[code // SHIFT])
            block = rights[code % SHIFT]
            parts_right += [block, block]
        product = jnp.dot(
            jnp.concatenate(parts_left, axis=1),
            jnp.concatenate(parts_right, axis=0),
            preferred_element_type=jnp.float32,
        )
        total[spot] += product[:, 0:size] + product[:, size : 2 * size]
        return 0

    half = slots // 2
    copies = []
    for part in range(2):
        lax.fori_loop(bound_ref[part], bound_ref[part + 1], multiply, 0)
        copies.append(
            pltpu.make_async_copy(
                total.at[pl.ds(part * half, half)], out_ref.at[pl.ds(part * half, half)], out_sem.at[part]
            )
        )
        copies[-1].start()
    for entry in copies:
        entry.wait()


def compute(plan, lefts, rights, own, slots):
    code, slot, bound = plan
    size = lefts[0].shape[-1]
    spans, sources = [], []
    for stop, array in enumerate(lefts):
        spans.append((0, stop * slots))
        sources.append(array)
    for array, base in rights:
        spans.append((1, base))
        sources.append(array)
    owners = 1 + max(base // own for _, base in rights)
    smem = pl.BlockSpec(memory_space=pltpu.SMEM)
    hbm = pl.BlockSpec(memory_space=pl.ANY)
    return pl.pallas_call(
        functools.partial(compute_body, spans, slots, own),
        out_shape=jax.ShapeDtypeStruct((slots, size, size), jnp.float32),
        in_specs=[smem] * 3 + [hbm] * len(sources),
        out_specs=hbm,
        scratch_shapes=[
            pltpu.VMEM((2 * slots + 1, size, 2 * size), jnp.bfloat16),
            pltpu.VMEM((owners * own, size, 2 * size), jnp.bfloat16),
            pltpu.VMEM((slots, size, size), jnp.float32),
            pltpu.VMEM((2, CHUNK, size, size), jnp.float32),
            pltpu.SemaphoreType.DMA((2,)),
            pltpu.SemaphoreType.DMA((2,)),
        ],
        compiler_params=pltpu.CompilerParams(vmem_limit_bytes=60 * 1024 * 1024),
        name="compute",
    )(code, slot, bound, *sources)


def local(left_blocks, right_blocks, left_send, left_place, right_send, right_place, triples):
    rows = lax.axis_size("row")
    cols = lax.axis_size("col")
    row = lax.axis_index("row").astype(jnp.int32)
    left_own = left_blocks[0, 0]
    right_own = right_blocks[0, 0]
    own = left_own.shape[0]
    size = left_own.shape[-1]
    left_list = left_send[0, 0]
    right_list = right_send[0, 0]
    positions = left_place[0, 0]
    per_left, per_right = left_list.shape[1], right_list.shape[1]
    panel, pairs = positions.shape[1], triples.shape[-1]
    slots = cols * per_left
    sizes = (rows, cols, own, per_left, per_right, panel, pairs)

    masks = [1 << bit for bit in range((rows - 1).bit_length())]
    table_own = jnp.concatenate([right_list.reshape(-1), right_place[0, 0].reshape(-1)])
    tables = spread(table_own, "row", masks)
    table = jnp.stack([tables[mask] for mask in range(rows)])
    left_next = shifted(positions, "col", -1)

    middle = own // 2
    first = spread(right_own[:middle], "row", masks)
    second = spread(right_own[middle:], "row", masks[::-1])
    rights = []
    for mask in range(rows):
        rights.append((first[mask], mask * own))
        rights.append((second[mask], mask * own + middle))

    buckets = left_own[jnp.clip(left_list.reshape(-1), 0, own - 1)]
    left_here = lax.all_to_all(buckets, "col", split_axis=0, concat_axis=0, tiled=True)
    left_there = shifted(left_here, "col", -1)

    plan = make_plan(row[None], triples[0, 0], positions, left_next, table, sizes)
    product = compute(plan, [left_here, left_there], rights, own, slots)
    half = per_left // 2
    flat = left_list.reshape(-1)
    backs = [
        lax.all_to_all(product[part * (slots // 2) : (part + 1) * (slots // 2)], "col", 0, 0, tiled=True)
        for part in range(2)
    ]
    back = jnp.concatenate(backs)
    wanted = (flat[None, :] == jnp.arange(own, dtype=jnp.int32)[:, None])
    index = jnp.arange(slots, dtype=jnp.int32)
    within = index % per_left
    spots = (within // half) * (cols * half) + (index // per_left) * half + within % half
    origin = jnp.sum(jnp.where(wanted, spots[None, :], 0), axis=1)
    return back[origin][None, None]


def solution(mesh):
    placed = (
        P("row", "col", None, None, None),
        P("row", "col", None, None, None),
        P("row", "col", None, None),
        P("row", "col", None, None),
        P("row", "col", None, None),
        P("row", "col", None, None),
        P("row", "col", None, None, None, None),
    )
    return jax.shard_map(
        local,
        mesh=mesh,
        in_specs=placed,
        out_specs=P("row", "col", None, None, None),
        check_vma=False,
    )
```

```python
import functools

import jax
import jax.numpy as jnp
from jax import lax
from jax.experimental import pallas as pl
from jax.experimental.pallas import tpu as pltpu
from jax.sharding import PartitionSpec as P


GROUP = 4
UNROLL = 4
SHIFT = 1024
ABSENT = -(1 << 24)
LATE = 1 << 10
SMEM = pl.BlockSpec(memory_space=pltpu.SMEM)
HBM = pl.BlockSpec(memory_space=pl.ANY)


def moved(value, axis, target, among=None):
    places = range(lax.axis_size(axis)) if among is None else among
    return lax.ppermute(value, axis, [(source, target(source)) for source in places])


def spread(piece, axis, masks):
    held = {0: piece}
    for mask in masks:
        for key, value in list(held.items()):
            held[mask ^ key] = moved(value, axis, lambda source: source ^ mask)
    return held


def plan_body(sizes, place_ref, triple_ref, left_ref, left_next_ref, table_ref, code_ref, slot_ref, bound_ref,
              block_ref, left_at, right_at, out_at, raw_code, raw_key, count_ref):
    rows, cols, own, per_left, per_right, panel, pairs = sizes
    row, col = place_ref[0], place_ref[1]
    half = per_left // 2
    middle, quarter = cols // 2, cols // 4
    slots = cols * per_left
    stride = panel + 1

    for stop in range(2):
        for image in range(2):
            left_at[(stop * 2 + image) * stride] = ABSENT
            right_at[(stop * 2 + image) * stride] = ABSENT
            out_at[image * stride] = 2 * slots

    def tables(index, _):
        image = index // panel
        slot = lax.rem(index, panel)
        for stop in range(2):
            entry = (stop * 2 + image) * stride + 1 + slot
            left = (left_ref if stop == 0 else left_next_ref)[image, slot]
            safe = jnp.maximum(left, 0)
            owner, within = safe // per_left, lax.rem(safe, per_left)
            if stop == 0:
                bucket = owner ^ col
                spot = (within // half) * (cols * half) + bucket * half + lax.rem(within, half)
                out_at[image * stride + 1 + slot] = jnp.where(left >= 0, spot, 2 * slots)
            else:
                after = lax.rem(col + 1, cols)
                bucket = owner ^ after
                crossing = lax.rem(after, middle) == 0
                turned = jnp.where(bucket < quarter, bucket, bucket + middle)
                turned = jnp.where(bucket < middle, turned, quarter + (owner ^ col))
                bucket = jnp.where(crossing, turned, bucket)
            late = bucket >= 3 * quarter
            early_at = 1 + (stop * 3 * quarter + bucket) * per_left + within
            late_at = 1 + (stop * quarter + bucket - 3 * quarter) * per_left + within + LATE
            left_at[entry] = jnp.where(left >= 0, jnp.where(late, late_at, early_at) * SHIFT, ABSENT)
            target = lax.rem(row + stop, rows)
            turned = jnp.where(row == rows - 1, 1 - image, image) if stop == 1 else image
            place = table_ref[target ^ row, rows * per_right + turned * panel + slot]
            safe = jnp.maximum(place, 0)
            source = (safe // per_right) ^ row
            block = table_ref[source, target * per_right + lax.rem(safe, per_right)]
            there = (place >= 0) & (block >= 0)
            right_at[entry] = jnp.where(there, stop * 2 * panel + index, ABSENT)
            block_ref[stop * 2 * panel + index] = jnp.where(there, source * own + block, 0)
        return 0

    lax.fori_loop(0, 2 * panel, tables, 0)

    def clear(index, _):
        count_ref[index] = 0
        return 0

    lax.fori_loop(0, 2 * slots + 1, clear, 0)
    total = jnp.int32(0)
    for stop in range(2):
        for image in range(2):
            base = (stop * 2 + image) * stride + 1

            def read(index, found):
                a = triple_ref[image, stop, 0, index]
                b = triple_ref[image, stop, 1, index]
                t = triple_ref[image, stop, 2, index]
                code = left_at[base + a] + right_at[base + b]
                spot = out_at[image * stride + 1 + t]
                live = (code >= 0) & (spot < slots)
                late = (code >= LATE * SHIFT).astype(jnp.int32)
                key = jnp.where(live, spot + late * slots, 2 * slots)
                raw_code[found] = code - late * (LATE * SHIFT)
                raw_key[found] = key
                count_ref[key] = count_ref[key] + 1
                return found + live.astype(jnp.int32)

            total = lax.fori_loop(0, pairs, read, total, unroll=4)

    def fill(index, _):
        code_ref[index] = 0
        return 0

    lax.fori_loop(0, code_ref.shape[0], fill, 0, unroll=16)

    def idle(index, _):
        slot_ref[index] = slots
        return 0

    lax.fori_loop(0, slot_ref.shape[0], idle, 0, unroll=16)

    def prefix(key, group):
        groups = (count_ref[key] + GROUP - 1) // GROUP

        def label(index, _):
            slot_ref[index] = lax.rem(key, slots)
            return 0

        lax.fori_loop(group, group + groups, label, 0)
        count_ref[key] = group * GROUP
        return group + groups

    done = jnp.int32(0)
    bound_ref[0] = 0
    for part, (low, high) in enumerate([(0, slots), (slots, slots + slots // 2), (slots + slots // 2, 2 * slots)]):
        done = lax.fori_loop(low, high, prefix, done)
        done = (done + UNROLL - 1) // UNROLL * UNROLL
        bound_ref[part + 1] = done // UNROLL

    def place(index, _):
        key = raw_key[index]
        spot = count_ref[key]
        code_ref[spot] = raw_code[index]
        count_ref[key] = spot + 1
        return 0

    lax.fori_loop(0, total, place, 0)


def make_plan(place, triples, left_place, left_next, table, sizes):
    _, cols, _, per_left, _, panel, pairs = sizes
    slots = cols * per_left
    groups = 4 * pairs // GROUP + 2 * slots + 3 * UNROLL
    groups = (groups + 31) // 32 * 32
    return pl.pallas_call(
        functools.partial(plan_body, sizes),
        out_shape=(
            jax.ShapeDtypeStruct((groups * GROUP,), jnp.int32),
            jax.ShapeDtypeStruct((groups,), jnp.int32),
            jax.ShapeDtypeStruct((4,), jnp.int32),
            jax.ShapeDtypeStruct((4 * panel,), jnp.int32),
        ),
        in_specs=[SMEM] * 5,
        out_specs=(SMEM,) * 4,
        scratch_shapes=[
            pltpu.SMEM((4 * (panel + 1),), jnp.int32),
            pltpu.SMEM((4 * (panel + 1),), jnp.int32),
            pltpu.SMEM((2 * (panel + 1),), jnp.int32),
            pltpu.SMEM((4 * pairs + 8,), jnp.int32),
            pltpu.SMEM((4 * pairs + 8,), jnp.int32),
            pltpu.SMEM((2 * slots + 8,), jnp.int32),
        ],
        cost_estimate=pl.CostEstimate(flops=40_000_000, bytes_accessed=60_000_000, transcendentals=0),
        name="plan",
    )(place, triples, left_place, left_next, table)


def halves(value):
    high = value.astype(jnp.bfloat16)
    return high, (value - high.astype(jnp.float32)).astype(jnp.bfloat16)


DEPTH = 8
CHUNK = 8


def split_body(bases, *refs):
    sources, (out_ref, raw, cut, in_sems, out_sems) = refs[: len(bases)], refs[-5:]
    size = raw.shape[-1]
    steps = []
    for source, base in zip(sources, bases):
        for start in range(0, source.shape[0], CHUNK):
            steps.append((source, start, min(CHUNK, source.shape[0] - start), base + start))

    def fetch(step):
        source, start, count, _ = steps[step]
        slot = step % DEPTH
        return pltpu.make_async_copy(source.at[pl.ds(start, count)], raw.at[slot, pl.ds(0, count)], in_sems.at[slot])

    def store(step):
        _, _, count, base = steps[step]
        slot = step % DEPTH
        return pltpu.make_async_copy(cut.at[slot, pl.ds(0, count)], out_ref.at[pl.ds(base, count)], out_sems.at[slot])

    for step in range(min(DEPTH, len(steps))):
        fetch(step).start()
    for step in range(len(steps)):
        slot = step % DEPTH
        fetch(step).wait()
        if step >= DEPTH:
            store(step - DEPTH).wait()

        def convert(index, _):
            high, low = halves(raw[slot, index])
            cut[slot, index, :, 0:size] = high
            cut[slot, index, :, size : 2 * size] = low
            return 0

        lax.fori_loop(0, steps[step][2], convert, 0)
        store(step).start()
        if step + DEPTH < len(steps):
            fetch(step + DEPTH).start()
    for step in range(max(0, len(steps) - DEPTH), len(steps)):
        store(step).wait()


def split(pieces, count, held=None):
    size = pieces[0][0].shape[-1]
    held = [] if held is None else [held]
    return pl.pallas_call(
        functools.partial(split_body, [base for _, base in pieces]),
        out_shape=jax.ShapeDtypeStruct((count, size, 2 * size), jnp.bfloat16),
        in_specs=[HBM] * (len(pieces) + len(held)),
        out_specs=HBM,
        input_output_aliases={len(pieces): 0} if held else {},
        scratch_shapes=[
            pltpu.VMEM((DEPTH, CHUNK, size, size), jnp.float32),
            pltpu.VMEM((DEPTH, CHUNK, size, 2 * size), jnp.bfloat16),
            pltpu.SemaphoreType.DMA((DEPTH,)),
            pltpu.SemaphoreType.DMA((DEPTH,)),
        ],
        cost_estimate=pl.CostEstimate(flops=0, bytes_accessed=2 * count * size * size * 4, transcendentals=0),
        name="split",
    )(*[piece for piece, _ in pieces], *held)


def multiply_body(late, part, kinds, sizes, place_ref, code_ref, slot_ref, bound_ref, block_ref, right_ref, *refs):
    _, cols, _, per_left, _, panel, _ = sizes
    slots = cols * per_left
    half = per_left // 2
    spots = slots // 2 if late else slots
    outs = cols if late else 1
    count = len(kinds) + sum(kinds)
    sources, before_ref, rest = refs[:count], refs[count] if late else None, refs[count + late :]
    out_refs, (lefts, rights, total, raw, left_sems, right_sem, total_sem, out_sem) = rest[:outs], rest[outs:]
    size = raw.shape[-1]
    first = part * spots
    crossing = lax.rem(place_ref[1] + 1, cols // 2) == 0

    def fetch(source, bucket):
        return pltpu.make_async_copy(source, raw.at[pl.ds(bucket * per_left, per_left)], left_sems.at[bucket])

    def gather(index, _):
        block = block_ref[index]
        pltpu.make_async_copy(right_ref.at[block], rights.at[index], right_sem).start()
        return 0

    offset = 0
    for bucket, two in enumerate(kinds):
        if two:

            @pl.when(jnp.logical_not(crossing))
            def _():
                fetch(sources[offset], bucket).start()

            @pl.when(crossing)
            def _():
                fetch(sources[offset + 1], bucket).start()

        else:
            fetch(sources[offset], bucket).start()
        offset += 1 + two
    lax.fori_loop(0, 4 * panel, gather, 0, unroll=4)
    if late:
        carried = pltpu.make_async_copy(before_ref.at[pl.ds(first, spots)], total.at[pl.ds(0, spots)], total_sem)
        carried.start()
        total[spots] = jnp.zeros(total.shape[1:], total.dtype)
    else:
        total[...] = jnp.zeros_like(total)
    lefts[0] = jnp.zeros(lefts.shape[1:], lefts.dtype)
    for bucket in range(len(kinds)):
        fetch(sources[0], bucket).wait()

        def convert(index, _):
            high, low = halves(raw[index])
            lefts[1 + index, :, 0:size] = high
            lefts[1 + index, :, size : 2 * size] = low
            return 0

        lax.fori_loop(bucket * per_left, (bucket + 1) * per_left, convert, 0, unroll=2)
    pltpu.make_async_copy(right_ref.at[pl.ds(0, 4 * panel)], rights, right_sem).wait()
    if late:
        carried.wait()

    def multiply(step, _):
        for lane in range(UNROLL):
            group = step * UNROLL + lane
            spot = jnp.minimum(slot_ref[group] - first, spots)
            parts_left, parts_right = [], []
            for index in range(GROUP):
                code = code_ref[group * GROUP + index]
                parts_left.append(lefts[code // SHIFT])
                block = rights[lax.rem(code, SHIFT)]
                parts_right += [block, block]
            product = jnp.dot(
                jnp.concatenate(parts_left, axis=1),
                jnp.concatenate(parts_right, axis=0),
                preferred_element_type=jnp.float32,
            )
            total[spot] += product[:, 0:size] + product[:, size : 2 * size]
        return 0

    chapter = 1 + part if late else 0
    lax.fori_loop(bound_ref[chapter], bound_ref[chapter + 1], multiply, 0)
    copies = []
    if late:
        for bucket in range(cols):
            copies.append(
                pltpu.make_async_copy(total.at[pl.ds(bucket * half, half)], out_refs[bucket], out_sem.at[bucket])
            )
    else:
        copies.append(pltpu.make_async_copy(total.at[pl.ds(0, slots)], out_refs[0], out_sem.at[0]))
    for entry in copies:
        entry.start()
    for entry in copies:
        entry.wait()


def multiplied(late, part, sizes, place, plan, rights, lefts, before=None):
    _, cols, _, per_left, _, panel, _ = sizes
    slots = cols * per_left
    spots = slots // 2 if late else slots
    size = rights.shape[1]
    if late:
        out_shape = [jax.ShapeDtypeStruct((per_left // 2, size, size), jnp.float32)] * cols
        out_specs = [HBM] * cols
    else:
        out_shape, out_specs = jax.ShapeDtypeStruct((slots, size, size), jnp.float32), HBM
    arrays = [array for entry in lefts for array in entry] + ([before] if late else [])
    return pl.pallas_call(
        functools.partial(multiply_body, late, part, [len(entry) - 1 for entry in lefts], sizes),
        out_shape=out_shape,
        in_specs=[SMEM] * 5 + [HBM] * (1 + len(arrays)),
        out_specs=out_specs,
        scratch_shapes=[
            pltpu.VMEM((len(lefts) * per_left + 1, size, 2 * size), jnp.bfloat16),
            pltpu.VMEM((4 * panel, size, 2 * size), jnp.bfloat16),
            pltpu.VMEM((spots + 1, size, size), jnp.float32),
            pltpu.VMEM((len(lefts) * per_left, size, size), jnp.float32),
            pltpu.SemaphoreType.DMA((len(lefts),)),
            pltpu.SemaphoreType.DMA,
            pltpu.SemaphoreType.DMA,
            pltpu.SemaphoreType.DMA((cols,)),
        ],
        cost_estimate=pl.CostEstimate(flops=0, bytes_accessed=4 * slots * size * size * 4, transcendentals=0),
        compiler_params=pltpu.CompilerParams(vmem_limit_bytes=40 * 1024 * 1024),
    )(place, *plan, rights, *arrays)


def collect_body(sizes, place_ref, list_ref, *refs):
    _, cols, _, per_left, _, _, _ = sizes
    half = per_left // 2
    sources, out_ref, whole, sem, out_sem = refs[: 2 * cols], *refs[2 * cols :]
    for part in range(2):
        for bucket in range(cols):
            for within in range(half):
                block = list_ref[place_ref[1] ^ bucket, part * half + within]

                @pl.when(block >= 0)
                def _():
                    pltpu.make_async_copy(sources[part * cols + bucket].at[within], whole.at[block], sem).start()

    pltpu.make_async_copy(out_ref, whole, sem).wait()
    result = pltpu.make_async_copy(whole, out_ref, out_sem)
    result.start()
    result.wait()


def collected(sizes, place, left_list, backs):
    own, size = sizes[2], backs[0].shape[-1]
    return pl.pallas_call(
        functools.partial(collect_body, sizes),
        out_shape=jax.ShapeDtypeStruct((own, size, size), jnp.float32),
        in_specs=[SMEM] * 2 + [HBM] * len(backs),
        out_specs=HBM,
        scratch_shapes=[
            pltpu.VMEM((own, size, size), jnp.float32),
            pltpu.SemaphoreType.DMA,
            pltpu.SemaphoreType.DMA,
        ],
        name="collect",
    )(place, left_list, *backs)


def local(left_blocks, right_blocks, left_send, left_place, right_send, right_place, triples):
    rows, cols = lax.axis_size("row"), lax.axis_size("col")
    row, col = lax.axis_index("row").astype(jnp.int32), lax.axis_index("col").astype(jnp.int32)
    place = jnp.stack([row, col])
    left_own, right_own = left_blocks[0, 0], right_blocks[0, 0]
    own = left_own.shape[0]
    left_list, right_list = left_send[0, 0], right_send[0, 0]
    positions = left_place[0, 0]
    per_left, per_right = left_list.shape[1], right_list.shape[1]
    panel, pairs = positions.shape[1], triples.shape[-1]
    sizes = (rows, cols, own, per_left, per_right, panel, pairs)
    middle, quarter = cols // 2, cols // 4
    back_one = lambda source: (source - 1) % cols

    masks = [1 << bit for bit in range((rows - 1).bit_length())]
    table_own = jnp.concatenate([right_list.reshape(-1), right_place[0, 0].reshape(-1)])
    tables = spread(table_own, "row", masks)
    table = jnp.stack([tables[mask] for mask in range(rows)])
    left_next = moved(positions, "col", back_one)

    cut = own // 2
    whole, low, high = {0: right_own}, {}, {}
    for mask in masks:
        whole[mask] = moved(right_own, "row", lambda source: source ^ mask)
        low[mask], high[mask] = whole[mask][:cut], whole[mask][cut:]
    for key in range(rows):
        if key not in whole:
            top, bottom = 1 << (key.bit_length() - 1), key & -key
            low[key] = moved(low[key ^ top], "row", lambda source: source ^ top)
            high[key] = moved(high[key ^ bottom], "row", lambda source: source ^ bottom)

    def bucket_for(peer):
        return left_own[jnp.clip(left_list[peer], 0, own - 1)]

    here = {0: bucket_for(col)}
    for mask in range(1, cols):
        here[mask] = moved(bucket_for(col ^ mask), "col", lambda source: source ^ mask)
    extra = {0: bucket_for(jnp.where(col < middle, middle, 0))}
    for mask in range(1, middle):
        extra[mask] = moved(
            extra[0], "col", lambda source: source ^ mask, [(middle - 1) ^ mask, (cols - 1) ^ mask]
        )
    there = {}
    for mask in range(cols):
        among = None if mask < middle else [source for source in range(cols) if source % middle != 0]
        there[mask] = moved(here[mask], "col", back_one, among)

    plan = make_plan(place, triples[0, 0], positions, left_next, table, sizes)
    rights = split([(whole[mask], mask * own) for mask in whole], rows * own)
    pieces = []
    for mask in range(rows):
        if mask not in whole:
            pieces += [(low[mask], mask * own), (high[mask], mask * own + cut)]
    rights = split(pieces, rows * own, rights)
    early = [(here[mask],) for mask in range(3 * quarter)]
    early += [(there[mask],) for mask in range(quarter)]
    early += [(there[mask], extra[mask - quarter]) for mask in range(quarter, 3 * quarter)]
    late = [(here[mask],) for mask in range(3 * quarter, cols)]
    late += [(there[mask], there[mask - middle]) for mask in range(3 * quarter, cols)]
    before = multiplied(0, 0, sizes, place, plan, rights, early)
    backs = []
    for part in range(2):
        product = multiplied(1, part, sizes, place, plan, rights, late, before)
        returned = {0: product[0]}
        for mask in list(range(middle, cols)) + list(range(1, middle)):
            returned[mask] = moved(product[mask], "col", lambda source: source ^ mask)
        backs += [returned[mask] for mask in range(cols)]
    return collected(sizes, place, left_list, backs)[None, None]


def solution(mesh):
    placed = (
        P("row", "col", None, None, None),
        P("row", "col", None, None, None),
        P("row", "col", None, None),
        P("row", "col", None, None),
        P("row", "col", None, None),
        P("row", "col", None, None),
        P("row", "col", None, None, None, None),
    )

    return jax.shard_map(
        local,
        mesh=mesh,
        in_specs=placed,
        out_specs=P("row", "col", None, None, None),
        check_vma=False,
    )
```

```python
import functools

import jax
import jax.numpy as jnp
from jax import lax
from jax.experimental import pallas as pl
from jax.experimental.pallas import tpu as pltpu
from jax.sharding import PartitionSpec as P


GROUP = 4
UNROLL = 4
SHIFT = 1024
READ = 8
ABSENT = -(1 << 24)
LATE = 20
RELAY = 21
SMEM = pl.BlockSpec(memory_space=pltpu.SMEM)
HBM = pl.BlockSpec(memory_space=pl.ANY)


def moved(value, axis, target, among=None):
    places = range(lax.axis_size(axis)) if among is None else among
    return lax.ppermute(value, axis, [(source, target(source)) for source in places])


def spread(piece, axis, masks):
    held = {0: piece}
    for mask in masks:
        for key, value in list(held.items()):
            held[mask ^ key] = moved(value, axis, lambda source: source ^ mask)
    return held


def right_order(rows):
    direct = [0] + [1 << bit for bit in range((rows - 1).bit_length())]
    return direct + [mask for mask in range(rows) if mask not in direct]


def plan_body(sizes, place_ref, triple_ref, left_ref, left_next_ref, table_ref, code_ref, slot_ref, bound_ref,
              block_ref, left_at, right_at, out_at, raw_code, raw_key, count_ref):
    rows, cols, own, per_left, per_right, panel, pairs = sizes
    row, col = place_ref[0], place_ref[1]
    half = per_left // 2
    middle, quarter = cols // 2, cols // 4
    slots = cols * per_left
    stride = panel + 1

    for stop in range(2):
        for image in range(2):
            left_at[(stop * 2 + image) * stride] = ABSENT
            right_at[(stop * 2 + image) * stride] = ABSENT
            out_at[image * stride] = slots

    def tables(index, _):
        image = index // panel
        slot = lax.rem(index, panel)
        for stop in range(2):
            entry = (stop * 2 + image) * stride + 1 + slot
            left = (left_ref if stop == 0 else left_next_ref)[image, slot]
            safe = jnp.maximum(left, 0)
            owner, within = safe // per_left, lax.rem(safe, per_left)
            if stop == 0:
                bucket = owner ^ col
                spot = (within // half) * (cols * half) + bucket * half + lax.rem(within, half)
                out_at[image * stride + 1 + slot] = jnp.where(left >= 0, spot, slots)
            else:
                after = lax.rem(col + 1, cols)
                bucket = owner ^ after
                crossing = lax.rem(after, middle) == 0
                turned = jnp.where(bucket < quarter, bucket, bucket + middle)
                turned = jnp.where(bucket < middle, turned, quarter + (owner ^ col))
                bucket = jnp.where(crossing, turned, bucket)
            late = bucket >= 3 * quarter
            early_at = (1 + (stop * 3 * quarter + bucket) * per_left + within) * SHIFT
            late_at = (1 + (stop * quarter + bucket - 3 * quarter) * per_left + within) * SHIFT + (1 << LATE)
            left_at[entry] = jnp.where(left >= 0, jnp.where(late, late_at, early_at), ABSENT)
            target = lax.rem(row + stop, rows)
            turned = jnp.where(row == rows - 1, 1 - image, image) if stop == 1 else image
            place = table_ref[target ^ row, rows * per_right + turned * panel + slot]
            safe = jnp.maximum(place, 0)
            source = (safe // per_right) ^ row
            block = table_ref[source, target * per_right + lax.rem(safe, per_right)]
            there = (place >= 0) & (block >= 0)
            rank = jnp.int32(0)
            for position, mask in enumerate(right_order(rows)):
                rank = jnp.where(source == mask, position, rank)
            relay = (rank >= rows.bit_length()).astype(jnp.int32) << RELAY
            right_at[entry] = jnp.where(there, stop * 2 * panel + index + relay, ABSENT)
            block_ref[stop * 2 * panel + index] = jnp.where(there, rank * own + block, 0)
        return 0

    lax.fori_loop(0, 2 * panel, tables, 0)

    def clear(index, _):
        count_ref[index] = 0
        return 0

    lax.fori_loop(0, 3 * slots + 1, clear, 0)
    total = jnp.int32(0)
    for stop in range(2):
        for image in range(2):
            base = (stop * 2 + image) * stride

            def read(step, found):
                codes, spots = [], []
                for lane in range(READ):
                    packed = triple_ref[(image * 2 + stop) * pairs + step * READ + lane]
                    codes.append(left_at[base + (packed & 255)] + right_at[base + ((packed >> 8) & 255)])
                    spots.append(out_at[image * stride + (packed >> 16)])
                for code, spot in zip(codes, spots):
                    live = (code >= 0) & (spot < slots)
                    chapter = (code >> RELAY) & 1 if stop == 0 else 1
                    chapter = jnp.where(((code >> LATE) & 1) == 1, 2, chapter)
                    key = jnp.where(live, spot + chapter * slots, 3 * slots)
                    raw_code[found] = code & ((1 << LATE) - 1)
                    raw_key[found] = key
                    count_ref[key] = count_ref[key] + 1
                    found = found + live.astype(jnp.int32)
                return found

            total = lax.fori_loop(0, pairs // READ, read, total)

    def fill(index, _):
        code_ref[index] = 0
        return 0

    lax.fori_loop(0, code_ref.shape[0], fill, 0, unroll=16)

    def idle(index, _):
        slot_ref[index] = slots
        return 0

    lax.fori_loop(0, slot_ref.shape[0], idle, 0, unroll=16)

    def prefix(key, group):
        groups = (count_ref[key] + GROUP - 1) // GROUP

        def label(index, _):
            slot_ref[index] = lax.rem(key, slots)
            return 0

        lax.fori_loop(group, group + groups, label, 0)
        count_ref[key] = group * GROUP
        return group + groups

    done = jnp.int32(0)
    bound_ref[0] = 0
    cuts = (0, slots, 2 * slots, 2 * slots + slots // 2, 3 * slots)
    for part, (low, high) in enumerate(zip(cuts[:-1], cuts[1:])):
        done = lax.fori_loop(low, high, prefix, done)
        done = (done + UNROLL - 1) // UNROLL * UNROLL
        bound_ref[part + 1] = done // UNROLL

    def place(index, _):
        key = raw_key[index]
        spot = count_ref[key]
        code_ref[spot] = raw_code[index]
        count_ref[key] = spot + 1
        return 0

    lax.fori_loop(0, total, place, 0)


def make_plan(place, triples, left_place, left_next, table, sizes):
    _, cols, _, per_left, _, panel, pairs = sizes
    slots = cols * per_left
    groups = 4 * pairs // GROUP + 3 * slots + 4 * UNROLL
    groups = (groups + 31) // 32 * 32
    return pl.pallas_call(
        functools.partial(plan_body, sizes),
        out_shape=(
            jax.ShapeDtypeStruct((groups * GROUP,), jnp.int32),
            jax.ShapeDtypeStruct((groups,), jnp.int32),
            jax.ShapeDtypeStruct((5,), jnp.int32),
            jax.ShapeDtypeStruct((4 * panel,), jnp.int32),
        ),
        in_specs=[SMEM] * 5,
        out_specs=(SMEM,) * 4,
        scratch_shapes=[
            pltpu.SMEM((4 * (panel + 1),), jnp.int32),
            pltpu.SMEM((4 * (panel + 1),), jnp.int32),
            pltpu.SMEM((2 * (panel + 1),), jnp.int32),
            pltpu.SMEM((4 * pairs + 8,), jnp.int32),
            pltpu.SMEM((4 * pairs + 8,), jnp.int32),
            pltpu.SMEM((3 * slots + 8,), jnp.int32),
        ],
        cost_estimate=pl.CostEstimate(flops=40_000_000, bytes_accessed=60_000_000, transcendentals=0),
        name="plan",
    )(place, triples, left_place, left_next, table)


def halves(value):
    high = value.astype(jnp.bfloat16)
    return high, (value - high.astype(jnp.float32)).astype(jnp.bfloat16)


DEPTH = 8
CHUNK = 8


def split_body(bases, *refs):
    sources, (out_ref, raw, cut, in_sems, out_sems) = refs[: len(bases)], refs[-5:]
    size = raw.shape[-1]
    steps = []
    for source, base in zip(sources, bases):
        for start in range(0, source.shape[0], CHUNK):
            steps.append((source, start, min(CHUNK, source.shape[0] - start), base + start))

    def fetch(step):
        source, start, count, _ = steps[step]
        slot = step % DEPTH
        return pltpu.make_async_copy(source.at[pl.ds(start, count)], raw.at[slot, pl.ds(0, count)], in_sems.at[slot])

    def store(step):
        _, _, count, base = steps[step]
        slot = step % DEPTH
        return pltpu.make_async_copy(cut.at[slot, pl.ds(0, count)], out_ref.at[pl.ds(base, count)], out_sems.at[slot])

    for step in range(min(DEPTH, len(steps))):
        fetch(step).start()
    for step in range(len(steps)):
        slot = step % DEPTH
        fetch(step).wait()
        if step >= DEPTH:
            store(step - DEPTH).wait()

        def convert(index, _):
            high, low = halves(raw[slot, index])
            cut[slot, index, :, 0:size] = high
            cut[slot, index, :, size : 2 * size] = low
            return 0

        lax.fori_loop(0, steps[step][2], convert, 0)
        store(step).start()
        if step + DEPTH < len(steps):
            fetch(step + DEPTH).start()
    for step in range(max(0, len(steps) - DEPTH), len(steps)):
        store(step).wait()


def split(pieces, count):
    size = pieces[0][0].shape[-1]
    return pl.pallas_call(
        functools.partial(split_body, [base for _, base in pieces]),
        out_shape=jax.ShapeDtypeStruct((count, size, 2 * size), jnp.bfloat16),
        in_specs=[HBM] * len(pieces),
        out_specs=HBM,
        scratch_shapes=[
            pltpu.VMEM((DEPTH, CHUNK, size, size), jnp.float32),
            pltpu.VMEM((DEPTH, CHUNK, size, 2 * size), jnp.bfloat16),
            pltpu.SemaphoreType.DMA((DEPTH,)),
            pltpu.SemaphoreType.DMA((DEPTH,)),
        ],
        cost_estimate=pl.CostEstimate(flops=0, bytes_accessed=2 * count * size * size * 4, transcendentals=0),
        name="split",
    )(*[piece for piece, _ in pieces])


def multiply_body(mode, part, kinds, sizes, place_ref, code_ref, slot_ref, bound_ref, block_ref, right_ref, *refs):
    _, cols, _, per_left, _, _, _ = sizes
    slots = cols * per_left
    half = per_left // 2
    relay_ref, refs = (refs[0], refs[1:]) if mode > 0 else (None, refs)
    direct = right_ref.shape[0]
    late, added = mode == 2, mode > 0
    spots = slots // 2 if late else slots
    outs = cols if late else 1
    count = len(kinds) + sum(kinds)
    sources, before_ref, rest = refs[:count], refs[count] if added else None, refs[count + added :]
    out_refs, (lefts, rights, total, raw, left_sems, right_sem, total_sem, out_sem) = rest[:outs], rest[outs:]
    size = raw.shape[-1]
    first = part * spots
    crossing = lax.rem(place_ref[1] + 1, cols // 2) == 0

    def fetch(source, bucket):
        return pltpu.make_async_copy(source, raw.at[pl.ds(bucket * per_left, per_left)], left_sems.at[bucket])

    def gather(index, _):
        block = block_ref[index]

        @pl.when(block < direct)
        def _():
            pltpu.make_async_copy(right_ref.at[block], rights.at[index], right_sem).start()

        @pl.when(block >= direct)
        def _():
            source = right_ref.at[0] if relay_ref is None else relay_ref.at[block - direct]
            pltpu.make_async_copy(source, rights.at[index], right_sem).start()

        return 0

    offset = 0
    for bucket, two in enumerate(kinds):
        if two:

            @pl.when(jnp.logical_not(crossing))
            def _():
                fetch(sources[offset], bucket).start()

            @pl.when(crossing)
            def _():
                fetch(sources[offset + 1], bucket).start()

        else:
            fetch(sources[offset], bucket).start()
        offset += 1 + two
    lax.fori_loop(0, rights.shape[0], gather, 0, unroll=4)
    if added:
        carried = pltpu.make_async_copy(before_ref.at[pl.ds(first, spots)], total.at[pl.ds(0, spots)], total_sem)
        carried.start()
        total[spots] = jnp.zeros(total.shape[1:], total.dtype)
    else:
        total[...] = jnp.zeros_like(total)
    lefts[0] = jnp.zeros(lefts.shape[1:], lefts.dtype)
    for bucket in range(len(kinds)):
        fetch(sources[0], bucket).wait()

        def convert(index, _):
            high, low = halves(raw[index])
            lefts[1 + index, :, 0:size] = high
            lefts[1 + index, :, size : 2 * size] = low
            return 0

        lax.fori_loop(bucket * per_left, (bucket + 1) * per_left, convert, 0, unroll=2)
    pltpu.make_async_copy(rights, rights, right_sem).wait()
    if added:
        carried.wait()

    def multiply(step, _):
        for lane in range(UNROLL):
            group = step * UNROLL + lane
            spot = jnp.minimum(slot_ref[group] - first, spots)
            parts_left, parts_right = [], []
            for index in range(GROUP):
                code = code_ref[group * GROUP + index]
                parts_left.append(lefts[code // SHIFT])
                block = rights[lax.rem(code, SHIFT)]
                parts_right += [block, block]
            product = jnp.dot(
                jnp.concatenate(parts_left, axis=1),
                jnp.concatenate(parts_right, axis=0),
                preferred_element_type=jnp.float32,
            )
            total[spot] += product[:, 0:size] + product[:, size : 2 * size]
        return 0

    chapter = mode + part
    lax.fori_loop(bound_ref[chapter], bound_ref[chapter + 1], multiply, 0)
    copies = []
    if late:
        for bucket in range(cols):
            copies.append(
                pltpu.make_async_copy(total.at[pl.ds(bucket * half, half)], out_refs[bucket], out_sem.at[bucket])
            )
    else:
        copies.append(pltpu.make_async_copy(total.at[pl.ds(0, slots)], out_refs[0], out_sem.at[0]))
    for entry in copies:
        entry.start()
    for entry in copies:
        entry.wait()


def multiplied(mode, part, sizes, place, plan, rights, lefts, before=None):
    _, cols, _, per_left, _, panel, _ = sizes
    slots = cols * per_left
    late = mode == 2
    spots = slots // 2 if late else slots
    size = rights[0].shape[1]
    rights = rights[: 1 + (mode > 0)]
    if late:
        out_shape = [jax.ShapeDtypeStruct((per_left // 2, size, size), jnp.float32)] * cols
        out_specs = [HBM] * cols
    else:
        out_shape, out_specs = jax.ShapeDtypeStruct((slots, size, size), jnp.float32), HBM
    arrays = [array for entry in lefts for array in entry] + ([before] if mode > 0 else [])
    return pl.pallas_call(
        functools.partial(multiply_body, mode, part, [len(entry) - 1 for entry in lefts], sizes),
        out_shape=out_shape,
        in_specs=[SMEM] * 5 + [HBM] * (len(rights) + len(arrays)),
        out_specs=out_specs,
        scratch_shapes=[
            pltpu.VMEM((len(lefts) * per_left + 1, size, 2 * size), jnp.bfloat16),
            pltpu.VMEM(((4 if mode > 0 else 2) * panel, size, 2 * size), jnp.bfloat16),
            pltpu.VMEM((spots + 1, size, size), jnp.float32),
            pltpu.VMEM((len(lefts) * per_left, size, size), jnp.float32),
            pltpu.SemaphoreType.DMA((len(lefts),)),
            pltpu.SemaphoreType.DMA,
            pltpu.SemaphoreType.DMA,
            pltpu.SemaphoreType.DMA((cols,)),
        ],
        cost_estimate=pl.CostEstimate(flops=0, bytes_accessed=4 * slots * size * size * 4, transcendentals=0),
        compiler_params=pltpu.CompilerParams(vmem_limit_bytes=48 * 1024 * 1024),
    )(place, *plan, *rights, *arrays)


def collect_body(sizes, place_ref, list_ref, *refs):
    _, cols, _, per_left, _, _, _ = sizes
    half = per_left // 2
    sources, out_ref, whole, sem, out_sem = refs[: 2 * cols], *refs[2 * cols :]
    for part in range(2):
        for bucket in range(cols):
            for within in range(half):
                block = list_ref[place_ref[1] ^ bucket, part * half + within]

                @pl.when(block >= 0)
                def _():
                    pltpu.make_async_copy(sources[part * cols + bucket].at[within], whole.at[block], sem).start()

    pltpu.make_async_copy(out_ref, whole, sem).wait()
    result = pltpu.make_async_copy(whole, out_ref, out_sem)
    result.start()
    result.wait()


def collected(sizes, place, left_list, backs):
    own, size = sizes[2], backs[0].shape[-1]
    return pl.pallas_call(
        functools.partial(collect_body, sizes),
        out_shape=jax.ShapeDtypeStruct((own, size, size), jnp.float32),
        in_specs=[SMEM] * 2 + [HBM] * len(backs),
        out_specs=HBM,
        scratch_shapes=[
            pltpu.VMEM((own, size, size), jnp.float32),
            pltpu.SemaphoreType.DMA,
            pltpu.SemaphoreType.DMA,
        ],
        name="collect",
    )(place, left_list, *backs)


def send_order(cols):
    middle = cols // 2
    order = []
    for index in range(max(middle - 2, cols // 4)):
        order += [mask for mask in (2 + index, middle + index) if mask < (middle if mask < middle else 3 * cols // 4)]
    order = list(dict.fromkeys(order))
    return order + [mask for mask in range(1, cols) if mask not in order and mask > 1] + [1]


def local(left_blocks, right_blocks, left_send, left_place, right_send, right_place, triples):
    rows, cols = lax.axis_size("row"), lax.axis_size("col")
    row, col = lax.axis_index("row").astype(jnp.int32), lax.axis_index("col").astype(jnp.int32)
    place = jnp.stack([row, col])
    left_own, right_own = left_blocks[0, 0], right_blocks[0, 0]
    own = left_own.shape[0]
    left_list, right_list = left_send[0, 0], right_send[0, 0]
    positions = left_place[0, 0]
    per_left, per_right = left_list.shape[1], right_list.shape[1]
    panel, pairs = positions.shape[1], triples.shape[-1]
    sizes = (rows, cols, own, per_left, per_right, panel, pairs)
    middle, quarter = cols // 2, cols // 4
    back_one = lambda source: (source - 1) % cols

    masks = [1 << bit for bit in range((rows - 1).bit_length())]
    table_own = jnp.concatenate([right_list.reshape(-1), right_place[0, 0].reshape(-1)])
    tables = spread(table_own, "row", masks)
    table = jnp.stack([tables[mask] for mask in range(rows)])
    left_next = moved(positions, "col", back_one)

    cut = own // 2
    whole, low, high = {0: right_own}, {}, {}
    for mask in masks:
        whole[mask] = moved(right_own, "row", lambda source: source ^ mask)
        low[mask], high[mask] = whole[mask][:cut], whole[mask][cut:]
    for key in range(rows):
        if key not in whole:
            top, bottom = 1 << (key.bit_length() - 1), key & -key
            low[key] = moved(low[key ^ top], "row", lambda source: source ^ top)
            high[key] = moved(high[key ^ bottom], "row", lambda source: source ^ bottom)

    def bucket_for(peer):
        return left_own[jnp.clip(left_list[peer], 0, own - 1)]

    here = {}
    for mask in send_order(cols):
        bucket = bucket_for(col ^ mask)
        here[mask] = moved(bucket, "col", lambda source: source ^ mask)
    here[0] = bucket_for(col)
    extra = {0: bucket_for(jnp.where(col < middle, middle, 0))}
    for mask in range(1, middle):
        extra[mask] = moved(
            extra[0], "col", lambda source: source ^ mask, [(middle - 1) ^ mask, (cols - 1) ^ mask]
        )
    there = {}
    for mask in range(cols):
        among = None if mask < middle else [source for source in range(cols) if source % middle != 0]
        there[mask] = moved(here[mask], "col", back_one, among)

    shifted = triples[0, 0] + 1
    packed = (shifted[:, :, 0] + shifted[:, :, 1] * 256 + shifted[:, :, 2] * 65536).reshape(-1)
    plan = make_plan(place, packed, positions, left_next, table, sizes)
    direct = split([(whole[mask], index * own) for index, mask in enumerate(whole)], len(whole) * own)
    pieces = []
    for index, mask in enumerate(right_order(rows)[len(whole) :]):
        pieces += [(low[mask], index * own), (high[mask], index * own + cut)]
    relayed = split(pieces, (rows - len(whole)) * own)
    rights = (direct, relayed)
    first = [(here[mask],) for mask in range(3 * quarter)]
    second = first + [(there[mask],) for mask in range(quarter)]
    second += [(there[mask], extra[mask - quarter]) for mask in range(quarter, 3 * quarter)]
    late = [(here[mask],) for mask in range(3 * quarter, cols)]
    late += [(there[mask], there[mask - middle]) for mask in range(3 * quarter, cols)]
    before = multiplied(0, 0, sizes, place, plan, rights, first)
    before = multiplied(1, 0, sizes, place, plan, rights, second, before)
    backs = []
    for part in range(2):
        product = multiplied(2, part, sizes, place, plan, rights, late, before)
        returned = {0: product[0]}
        for mask in list(range(middle, cols)) + list(range(1, middle)):
            returned[mask] = moved(product[mask], "col", lambda source: source ^ mask)
        backs += [returned[mask] for mask in range(cols)]
    return collected(sizes, place, left_list, backs)[None, None]


def solution(mesh):
    placed = (
        P("row", "col", None, None, None),
        P("row", "col", None, None, None),
        P("row", "col", None, None),
        P("row", "col", None, None),
        P("row", "col", None, None),
        P("row", "col", None, None),
        P("row", "col", None, None, None, None),
    )

    return jax.shard_map(
        local,
        mesh=mesh,
        in_specs=placed,
        out_specs=P("row", "col", None, None, None),
        check_vma=False,
    )
```

```python
import functools

import jax
import jax.numpy as jnp
from jax import lax
from jax.experimental import pallas as pl
from jax.experimental.pallas import tpu as pltpu
from jax.sharding import PartitionSpec as P


GROUP = 4
UNROLL = 4
SHIFT = 1024
READ = 8
ABSENT = -(1 << 24)
LATE = 20
RELAY = 21
SMEM = pl.BlockSpec(memory_space=pltpu.SMEM)
HBM = pl.BlockSpec(memory_space=pl.ANY)


def moved(value, axis, target, among=None):
    places = range(lax.axis_size(axis)) if among is None else among
    return lax.ppermute(value, axis, [(source, target(source)) for source in places])


def spread(piece, axis, masks):
    held = {0: piece}
    for mask in masks:
        for key, value in list(held.items()):
            held[mask ^ key] = moved(value, axis, lambda source: source ^ mask)
    return held


def right_order(rows):
    direct = [0] + [1 << bit for bit in range((rows - 1).bit_length())]
    return direct + [mask for mask in range(rows) if mask not in direct]


def plan_body(sizes, place_ref, triple_ref, left_ref, left_next_ref, table_ref, code_ref, bound_ref,
              block_ref, left_at, right_at, out_at, raw_code, raw_key, count_ref):
    rows, cols, own, per_left, per_right, panel, pairs = sizes
    row, col = place_ref[0], place_ref[1]
    half = per_left // 2
    middle, quarter = cols // 2, cols // 4
    slots = cols * per_left
    stride = panel + 1

    for stop in range(2):
        for image in range(2):
            left_at[(stop * 2 + image) * stride] = ABSENT
            right_at[(stop * 2 + image) * stride] = ABSENT
            out_at[image * stride] = slots

    def tables(index, _):
        image = index // panel
        slot = lax.rem(index, panel)
        for stop in range(2):
            entry = (stop * 2 + image) * stride + 1 + slot
            left = (left_ref if stop == 0 else left_next_ref)[image, slot]
            safe = jnp.maximum(left, 0)
            owner, within = safe // per_left, lax.rem(safe, per_left)
            if stop == 0:
                bucket = owner ^ col
                spot = (within // half) * (cols * half) + bucket * half + lax.rem(within, half)
                out_at[image * stride + 1 + slot] = jnp.where(left >= 0, spot, slots)
            else:
                after = lax.rem(col + 1, cols)
                bucket = owner ^ after
                crossing = lax.rem(after, middle) == 0
                turned = jnp.where(bucket < quarter, bucket, bucket + middle)
                turned = jnp.where(bucket < middle, turned, quarter + (owner ^ col))
                bucket = jnp.where(crossing, turned, bucket)
            late = bucket >= 3 * quarter
            early_at = (1 + (stop * 3 * quarter + bucket) * per_left + within) * SHIFT
            late_at = (1 + (stop * quarter + bucket - 3 * quarter) * per_left + within) * SHIFT + (1 << LATE)
            left_at[entry] = jnp.where(left >= 0, jnp.where(late, late_at, early_at), ABSENT)
            target = lax.rem(row + stop, rows)
            turned = jnp.where(row == rows - 1, 1 - image, image) if stop == 1 else image
            place = table_ref[target ^ row, rows * per_right + turned * panel + slot]
            safe = jnp.maximum(place, 0)
            source = (safe // per_right) ^ row
            block = table_ref[source, target * per_right + lax.rem(safe, per_right)]
            there = (place >= 0) & (block >= 0)
            rank = jnp.int32(0)
            for position, mask in enumerate(right_order(rows)):
                rank = jnp.where(source == mask, position, rank)
            relay = (rank >= rows.bit_length()).astype(jnp.int32) << RELAY
            right_at[entry] = jnp.where(there, stop * 2 * panel + index + relay, ABSENT)
            block_ref[stop * 2 * panel + index] = jnp.where(there, rank * own + block, 0)
        return 0

    lax.fori_loop(0, 2 * panel, tables, 0, unroll=2)

    def clear(index, _):
        count_ref[index] = 0
        return 0

    lax.fori_loop(0, 3 * slots + 8, clear, 0, unroll=8)
    total = jnp.int32(0)
    for stop in range(2):
        for image in range(2):
            base = (stop * 2 + image) * stride

            def read(step, found):
                codes, spots = [], []
                for lane in range(READ):
                    packed = triple_ref[(image * 2 + stop) * pairs + step * READ + lane]
                    codes.append(left_at[base + (packed & 255)] + right_at[base + ((packed >> 8) & 255)])
                    spots.append(out_at[image * stride + (packed >> 16)])
                for code, spot in zip(codes, spots):
                    live = (code >= 0) & (spot < slots)
                    chapter = (code >> RELAY) & 1 if stop == 0 else 1
                    chapter = jnp.where(((code >> LATE) & 1) == 1, 2, chapter)
                    key = jnp.where(live, spot + chapter * slots, 3 * slots)
                    raw_code[found] = (code & ((1 << LATE) - 1)) + (spot << LATE)
                    raw_key[found] = key
                    count_ref[key] = count_ref[key] + 1
                    found = found + live.astype(jnp.int32)
                return found

            total = lax.fori_loop(0, pairs // READ, read, total)

    def fill(index, _):
        code_ref[index] = slots << LATE
        return 0

    lax.fori_loop(0, code_ref.shape[0], fill, 0, unroll=16)

    def prefix(key, start):
        count = count_ref[key]
        count_ref[key] = start
        return start + (count + GROUP - 1) // GROUP * GROUP

    done = jnp.int32(0)
    bound_ref[0] = 0
    cuts = (0, slots, 2 * slots, 2 * slots + slots // 2, 3 * slots)
    for part, (low, high) in enumerate(zip(cuts[:-1], cuts[1:])):
        done = lax.fori_loop(low, high, prefix, done, unroll=8)
        done = (done + GROUP * UNROLL - 1) // (GROUP * UNROLL) * (GROUP * UNROLL)
        bound_ref[part + 1] = done // (GROUP * UNROLL)

    def place(index, _):
        key = raw_key[index]
        spot = count_ref[key]
        code_ref[spot] = raw_code[index]
        count_ref[key] = spot + 1
        return 0

    lax.fori_loop(0, total, place, 0)


def make_plan(place, triples, left_place, left_next, table, sizes):
    _, cols, _, per_left, _, panel, pairs = sizes
    slots = cols * per_left
    room = 4 * pairs + 3 * slots * (GROUP - 1) + 4 * GROUP * UNROLL
    room = (room + 127) // 128 * 128
    return pl.pallas_call(
        functools.partial(plan_body, sizes),
        out_shape=(
            jax.ShapeDtypeStruct((room,), jnp.int32),
            jax.ShapeDtypeStruct((5,), jnp.int32),
            jax.ShapeDtypeStruct((4 * panel,), jnp.int32),
        ),
        in_specs=[SMEM] * 5,
        out_specs=(SMEM,) * 3,
        scratch_shapes=[
            pltpu.SMEM((4 * (panel + 1),), jnp.int32),
            pltpu.SMEM((4 * (panel + 1),), jnp.int32),
            pltpu.SMEM((2 * (panel + 1),), jnp.int32),
            pltpu.SMEM((4 * pairs + 8,), jnp.int32),
            pltpu.SMEM((4 * pairs + 8,), jnp.int32),
            pltpu.SMEM((3 * slots + 8,), jnp.int32),
        ],
        cost_estimate=pl.CostEstimate(flops=40_000_000, bytes_accessed=60_000_000, transcendentals=0),
        name="plan",
    )(place, triples, left_place, left_next, table)


def halves(value):
    high = value.astype(jnp.bfloat16)
    return high, (value - high.astype(jnp.float32)).astype(jnp.bfloat16)


def take_body(masks, place_ref, list_ref, blocks_ref, *refs):
    outs, (held, in_sems, out_sems) = refs[: len(masks)], refs[len(masks) :]
    col = place_ref[1]
    cols, per_left = list_ref.shape
    for bucket, mask in enumerate(masks):
        peer = jnp.where(col < cols // 2, cols // 2, 0) if mask is None else col ^ mask
        for within in range(per_left):
            block = jnp.maximum(list_ref[peer, within], 0)
            pltpu.make_async_copy(blocks_ref.at[block], held.at[bucket, within], in_sems.at[bucket]).start()
    stores = []
    for bucket in range(len(masks)):
        pltpu.make_async_copy(held.at[bucket], held.at[bucket], in_sems.at[bucket]).wait()
        stores.append(pltpu.make_async_copy(held.at[bucket], outs[bucket], out_sems.at[bucket]))
        stores[-1].start()
    for store in stores:
        store.wait()


def take(masks, place, left_list, left_own):
    per_left, size = left_list.shape[1], left_own.shape[-1]
    return pl.pallas_call(
        functools.partial(take_body, masks),
        out_shape=[jax.ShapeDtypeStruct((per_left, size, size), jnp.float32)] * len(masks),
        in_specs=[SMEM] * 2 + [HBM],
        out_specs=[HBM] * len(masks),
        scratch_shapes=[
            pltpu.VMEM((len(masks), per_left, size, size), jnp.float32),
            pltpu.SemaphoreType.DMA((len(masks),)),
            pltpu.SemaphoreType.DMA((len(masks),)),
        ],
        compiler_params=pltpu.CompilerParams(vmem_limit_bytes=48 * 1024 * 1024),
        name="take",
    )(place, left_list, left_own)


def part_body(starts, *refs):
    count = len(starts)
    sources, outs, (held, in_sems, out_sems) = refs[:count], refs[count : 2 * count], refs[2 * count :]
    fetches, stores = [], []
    for index, start in enumerate(starts):
        length = outs[index].shape[0]
        target = held.at[index, pl.ds(0, length)]
        fetches.append(pltpu.make_async_copy(sources[index].at[pl.ds(start, length)], target, in_sems.at[index]))
        stores.append(pltpu.make_async_copy(target, outs[index], out_sems.at[index]))
    for fetch in fetches:
        fetch.start()
    for fetch, store in zip(fetches, stores):
        fetch.wait()
        store.start()
    for store in stores:
        store.wait()


def parted(wanted):
    size = wanted[0][0].shape[-1]
    longest = max(stop - start for _, start, stop in wanted)
    return pl.pallas_call(
        functools.partial(part_body, [start for _, start, _ in wanted]),
        out_shape=[jax.ShapeDtypeStruct((stop - start, size, size), jnp.float32) for _, start, stop in wanted],
        in_specs=[HBM] * len(wanted),
        out_specs=[HBM] * len(wanted),
        scratch_shapes=[
            pltpu.VMEM((len(wanted), longest, size, size), jnp.float32),
            pltpu.SemaphoreType.DMA((len(wanted),)),
            pltpu.SemaphoreType.DMA((len(wanted),)),
        ],
        compiler_params=pltpu.CompilerParams(vmem_limit_bytes=48 * 1024 * 1024),
        name="parted",
    )(*[array for array, _, _ in wanted])


DEPTH = 8
CHUNK = 8


def split_body(bases, *refs):
    sources, (out_ref, raw, cut, in_sems, out_sems) = refs[: len(bases)], refs[-5:]
    size = raw.shape[-1]
    steps = []
    for source, base in zip(sources, bases):
        for start in range(0, source.shape[0], CHUNK):
            steps.append((source, start, min(CHUNK, source.shape[0] - start), base + start))

    def fetch(step):
        source, start, count, _ = steps[step]
        slot = step % DEPTH
        return pltpu.make_async_copy(source.at[pl.ds(start, count)], raw.at[slot, pl.ds(0, count)], in_sems.at[slot])

    def store(step):
        _, _, count, base = steps[step]
        slot = step % DEPTH
        return pltpu.make_async_copy(cut.at[slot, pl.ds(0, count)], out_ref.at[pl.ds(base, count)], out_sems.at[slot])

    for step in range(min(DEPTH, len(steps))):
        fetch(step).start()
    for step in range(len(steps)):
        slot = step % DEPTH
        fetch(step).wait()
        if step >= DEPTH:
            store(step - DEPTH).wait()

        def convert(index, _):
            high, low = halves(raw[slot, index])
            cut[slot, index, :, 0:size] = high
            cut[slot, index, :, size : 2 * size] = low
            return 0

        lax.fori_loop(0, steps[step][2], convert, 0)
        store(step).start()
        if step + DEPTH < len(steps):
            fetch(step + DEPTH).start()
    for step in range(max(0, len(steps) - DEPTH), len(steps)):
        store(step).wait()


def split(pieces, count):
    size = pieces[0][0].shape[-1]
    return pl.pallas_call(
        functools.partial(split_body, [base for _, base in pieces]),
        out_shape=jax.ShapeDtypeStruct((count, size, 2 * size), jnp.bfloat16),
        in_specs=[HBM] * len(pieces),
        out_specs=HBM,
        scratch_shapes=[
            pltpu.VMEM((DEPTH, CHUNK, size, size), jnp.float32),
            pltpu.VMEM((DEPTH, CHUNK, size, 2 * size), jnp.bfloat16),
            pltpu.SemaphoreType.DMA((DEPTH,)),
            pltpu.SemaphoreType.DMA((DEPTH,)),
        ],
        cost_estimate=pl.CostEstimate(flops=0, bytes_accessed=2 * count * size * size * 4, transcendentals=0),
        name="split",
    )(*[piece for piece, _ in pieces])


def multiply_body(mode, part, kinds, sizes, place_ref, code_ref, bound_ref, block_ref, right_ref, *refs):
    _, cols, _, per_left, _, _, _ = sizes
    slots = cols * per_left
    half = per_left // 2
    relay_ref, refs = (refs[0], refs[1:]) if mode > 0 else (None, refs)
    direct = right_ref.shape[0]
    late, added = mode == 2, mode > 0
    spots = slots // 2 if late else slots
    outs = cols if late else 1
    count = len(kinds) + sum(kinds)
    sources, before_ref, rest = refs[:count], refs[count] if added else None, refs[count + added :]
    out_refs, (lefts, rights, total, raw, left_sems, right_sem, total_sem, out_sem) = rest[:outs], rest[outs:]
    size = raw.shape[-1]
    first = part * spots
    crossing = lax.rem(place_ref[1] + 1, cols // 2) == 0

    def fetch(source, bucket):
        return pltpu.make_async_copy(source, raw.at[pl.ds(bucket * per_left, per_left)], left_sems.at[bucket])

    def gather(index, _):
        block = block_ref[index]

        @pl.when(block < direct)
        def _():
            pltpu.make_async_copy(right_ref.at[block], rights.at[index], right_sem).start()

        @pl.when(block >= direct)
        def _():
            source = right_ref.at[0] if relay_ref is None else relay_ref.at[block - direct]
            pltpu.make_async_copy(source, rights.at[index], right_sem).start()

        return 0

    offset = 0
    for bucket, two in enumerate(kinds):
        if two:

            @pl.when(jnp.logical_not(crossing))
            def _():
                fetch(sources[offset], bucket).start()

            @pl.when(crossing)
            def _():
                fetch(sources[offset + 1], bucket).start()

        else:
            fetch(sources[offset], bucket).start()
        offset += 1 + two
    lax.fori_loop(0, rights.shape[0], gather, 0, unroll=4)
    if added:
        carried = pltpu.make_async_copy(before_ref.at[pl.ds(first, spots)], total.at[pl.ds(0, spots)], total_sem)
        carried.start()
        total[spots] = jnp.zeros(total.shape[1:], total.dtype)
    else:
        total[...] = jnp.zeros_like(total)
    lefts[0] = jnp.zeros(lefts.shape[1:], lefts.dtype)
    for bucket in range(len(kinds)):
        fetch(sources[0], bucket).wait()

        def convert(index, _):
            high, low = halves(raw[index])
            lefts[1 + index, :, 0:size] = high
            lefts[1 + index, :, size : 2 * size] = low
            return 0

        lax.fori_loop(bucket * per_left, (bucket + 1) * per_left, convert, 0, unroll=2)
    pltpu.make_async_copy(rights, rights, right_sem).wait()
    if added:
        carried.wait()

    def multiply(step, _):
        made = []
        for lane in range(UNROLL):
            start = (step * UNROLL + lane) * GROUP
            codes = [code_ref[start + index] for index in range(GROUP)]
            parts_left, parts_right = [], []
            for code in codes:
                parts_left.append(lefts[(code & ((1 << LATE) - 1)) // SHIFT])
                block = rights[code & (SHIFT - 1)]
                parts_right += [block, block]
            product = jnp.dot(
                jnp.concatenate(parts_left, axis=1),
                jnp.concatenate(parts_right, axis=0),
                preferred_element_type=jnp.float32,
            )
            made.append((jnp.minimum((codes[0] >> LATE) - first, spots), product))
        for spot, product in made:
            total[spot] += product[:, 0:size] + product[:, size : 2 * size]
        return 0

    chapter = mode + part
    lax.fori_loop(bound_ref[chapter], bound_ref[chapter + 1], multiply, 0)
    copies = []
    if late:
        for bucket in range(cols):
            copies.append(
                pltpu.make_async_copy(total.at[pl.ds(bucket * half, half)], out_refs[bucket], out_sem.at[bucket])
            )
    else:
        copies.append(pltpu.make_async_copy(total.at[pl.ds(0, slots)], out_refs[0], out_sem.at[0]))
    for entry in copies:
        entry.start()
    for entry in copies:
        entry.wait()


def multiplied(mode, part, sizes, place, plan, rights, lefts, before=None):
    _, cols, _, per_left, _, panel, _ = sizes
    slots = cols * per_left
    late = mode == 2
    spots = slots // 2 if late else slots
    size = rights[0].shape[1]
    rights = rights[: 1 + (mode > 0)]
    if late:
        out_shape = [jax.ShapeDtypeStruct((per_left // 2, size, size), jnp.float32)] * cols
        out_specs = [HBM] * cols
    else:
        out_shape, out_specs = jax.ShapeDtypeStruct((slots, size, size), jnp.float32), HBM
    arrays = [array for entry in lefts for array in entry] + ([before] if mode > 0 else [])
    return pl.pallas_call(
        functools.partial(multiply_body, mode, part, [len(entry) - 1 for entry in lefts], sizes),
        out_shape=out_shape,
        in_specs=[SMEM] * 4 + [HBM] * (len(rights) + len(arrays)),
        out_specs=out_specs,
        scratch_shapes=[
            pltpu.VMEM((len(lefts) * per_left + 1, size, 2 * size), jnp.bfloat16),
            pltpu.VMEM(((4 if mode > 0 else 2) * panel, size, 2 * size), jnp.bfloat16),
            pltpu.VMEM((spots + 1, size, size), jnp.float32),
            pltpu.VMEM((len(lefts) * per_left, size, size), jnp.float32),
            pltpu.SemaphoreType.DMA((len(lefts),)),
            pltpu.SemaphoreType.DMA,
            pltpu.SemaphoreType.DMA,
            pltpu.SemaphoreType.DMA((cols,)),
        ],
        cost_estimate=pl.CostEstimate(flops=0, bytes_accessed=4 * slots * size * size * 4, transcendentals=0),
        compiler_params=pltpu.CompilerParams(vmem_limit_bytes=48 * 1024 * 1024),
    )(place, *plan, *rights, *arrays)


def collect_body(part, sizes, place_ref, list_ref, *refs):
    _, cols, _, per_left, _, _, _ = sizes
    half = per_left // 2
    sources, (out_ref, held, in_sems, out_sems) = refs[:cols], refs[-4:]
    slots = [(bucket, within) for bucket in range(cols) for within in range(half)]

    def each(action):
        for index, (bucket, within) in enumerate(slots):
            block = list_ref[place_ref[1] ^ bucket, part * half + within]

            @pl.when(block >= 0)
            def _():
                action(
                    pltpu.make_async_copy(sources[bucket].at[within], held.at[index], in_sems.at[index]),
                    pltpu.make_async_copy(held.at[index], out_ref.at[block], out_sems.at[index]),
                )

    def forward(fetch, store):
        fetch.wait()
        store.start()

    each(lambda fetch, store: fetch.start())
    each(forward)
    each(lambda fetch, store: store.wait())


def collected(part, sizes, place, left_list, backs, before):
    _, cols, own, per_left, _, _, _ = sizes
    size = backs[0].shape[-1]
    slots = cols * per_left // 2
    held = [] if before is None else [before]
    return pl.pallas_call(
        functools.partial(collect_body, part, sizes),
        out_shape=jax.ShapeDtypeStruct((own, size, size), jnp.float32),
        in_specs=[SMEM] * 2 + [HBM] * (len(backs) + len(held)),
        out_specs=HBM,
        input_output_aliases={2 + len(backs): 0} if held else {},
        scratch_shapes=[
            pltpu.VMEM((slots, size, size), jnp.float32),
            pltpu.SemaphoreType.DMA((slots,)),
            pltpu.SemaphoreType.DMA((slots,)),
        ],
    )(place, left_list, *backs, *held)


def send_order(cols):
    middle = cols // 2
    order = []
    for index in range(max(middle - 2, cols // 4)):
        order += [mask for mask in (2 + index, middle + index) if mask < (middle if mask < middle else 3 * cols // 4)]
    order = list(dict.fromkeys(order))
    return order + [mask for mask in range(1, cols) if mask not in order and mask > 1] + [1]


def local(left_blocks, right_blocks, left_send, left_place, right_send, right_place, triples):
    rows, cols = lax.axis_size("row"), lax.axis_size("col")
    row, col = lax.axis_index("row").astype(jnp.int32), lax.axis_index("col").astype(jnp.int32)
    place = jnp.stack([row, col])
    left_own, right_own = left_blocks[0, 0], right_blocks[0, 0]
    own = left_own.shape[0]
    left_list, right_list = left_send[0, 0], right_send[0, 0]
    positions = left_place[0, 0]
    per_left, per_right = left_list.shape[1], right_list.shape[1]
    panel, pairs = positions.shape[1], triples.shape[-1]
    sizes = (rows, cols, own, per_left, per_right, panel, pairs)
    middle, quarter = cols // 2, cols // 4
    back_one = lambda source: (source - 1) % cols

    masks = [1 << bit for bit in range((rows - 1).bit_length())]
    table_own = jnp.concatenate([right_list.reshape(-1), right_place[0, 0].reshape(-1)])
    tables = spread(table_own, "row", masks)
    table = jnp.stack([tables[mask] for mask in range(rows)])
    left_next = moved(positions, "col", back_one)

    cut = own // 2
    whole, low, high = {0: right_own}, {}, {}
    for mask in masks:
        whole[mask] = moved(right_own, "row", lambda source: source ^ mask)
    relays = [(key, 1 << (key.bit_length() - 1), key & -key) for key in right_order(rows)[len(whole) :]]
    lows = sorted({key ^ top for key, top, _ in relays} & set(masks))
    highs = sorted({key ^ bottom for key, _, bottom in relays} & set(masks))
    parts = parted([(whole[mask], 0, cut) for mask in lows] + [(whole[mask], cut, own) for mask in highs])
    low.update(zip(lows, parts[: len(lows)]))
    high.update(zip(highs, parts[len(lows) :]))
    for key, top, bottom in relays:
        low[key] = moved(low[key ^ top], "row", lambda source: source ^ top)
        high[key] = moved(high[key ^ bottom], "row", lambda source: source ^ bottom)

    order = send_order(cols)
    taken = list(take(order[:2], place, left_list, left_own))
    taken += list(take(order[2:] + [0, None], place, left_list, left_own))
    here = {}
    for index, mask in enumerate(order):
        here[mask] = moved(taken[index], "col", lambda source: source ^ mask)
    here[0], extra = taken[-2], {0: taken[-1]}
    for mask in range(1, middle):
        extra[mask] = moved(
            extra[0], "col", lambda source: source ^ mask, [(middle - 1) ^ mask, (cols - 1) ^ mask]
        )
    there = {}
    for mask in range(cols):
        among = None if mask < middle else [source for source in range(cols) if source % middle != 0]
        there[mask] = moved(here[mask], "col", back_one, among)

    shifted = triples[0, 0] + 1
    packed = (shifted[:, :, 0] + shifted[:, :, 1] * 256 + shifted[:, :, 2] * 65536).reshape(-1)
    plan = make_plan(place, packed, positions, left_next, table, sizes)
    direct = split([(whole[mask], index * own) for index, mask in enumerate(whole)], len(whole) * own)
    pieces = []
    for index, mask in enumerate(right_order(rows)[len(whole) :]):
        pieces += [(low[mask], index * own), (high[mask], index * own + cut)]
    relayed = split(pieces, (rows - len(whole)) * own)
    rights = (direct, relayed)
    first = [(here[mask],) for mask in range(3 * quarter)]
    second = first + [(there[mask],) for mask in range(quarter)]
    second += [(there[mask], extra[mask - quarter]) for mask in range(quarter, 3 * quarter)]
    late = [(here[mask],) for mask in range(3 * quarter, cols)]
    late += [(there[mask], there[mask - middle]) for mask in range(3 * quarter, cols)]
    before = multiplied(0, 0, sizes, place, plan, rights, first)
    before = multiplied(1, 0, sizes, place, plan, rights, second, before)
    result = None
    backs = []
    for part in range(2):
        product = multiplied(2, part, sizes, place, plan, rights, late, before)
        returned = {0: product[0]}
        for mask in list(range(middle, cols)) + list(range(1, middle)):
            returned[mask] = moved(product[mask], "col", lambda source: source ^ mask)
        backs.append([returned[mask] for mask in range(cols)])
    for part in range(2):
        result = collected(part, sizes, place, left_list, backs[part], result)
    return result[None, None]


def solution(mesh):
    placed = (
        P("row", "col", None, None, None),
        P("row", "col", None, None, None),
        P("row", "col", None, None),
        P("row", "col", None, None),
        P("row", "col", None, None),
        P("row", "col", None, None),
        P("row", "col", None, None, None, None),
    )

    return jax.shard_map(
        local,
        mesh=mesh,
        in_specs=placed,
        out_specs=P("row", "col", None, None, None),
        check_vma=False,
    )
```

```python
import functools

import jax
import jax.numpy as jnp
from jax import lax
from jax.experimental import pallas as pl
from jax.experimental.pallas import tpu as pltpu
from jax.sharding import PartitionSpec as P


GROUP = 4
UNROLL = 8
SHIFT = 1024
READ = 8
ABSENT = -(1 << 24)
LATE = 20
RELAY = 21
SMEM = pl.BlockSpec(memory_space=pltpu.SMEM)
HBM = pl.BlockSpec(memory_space=pl.ANY)


def moved(value, axis, target, among=None):
    places = range(lax.axis_size(axis)) if among is None else among
    return lax.ppermute(value, axis, [(source, target(source)) for source in places])


def spread(piece, axis, masks):
    held = {0: piece}
    for mask in masks:
        for key, value in list(held.items()):
            held[mask ^ key] = moved(value, axis, lambda source: source ^ mask)
    return held


def right_order(rows):
    direct = [0] + [1 << bit for bit in range((rows - 1).bit_length())]
    return direct + [mask for mask in range(rows) if mask not in direct]


def plan_body(sizes, place_ref, triple_ref, left_ref, left_next_ref, table_ref, code_ref, bound_ref,
              block_ref, left_at, right_at, out_at, raw_code, raw_key, count_ref):
    rows, cols, own, per_left, per_right, panel, pairs = sizes
    row, col = place_ref[0], place_ref[1]
    half = per_left // 2
    middle, quarter = cols // 2, cols // 4
    slots = cols * per_left
    stride = panel + 1

    for stop in range(2):
        for image in range(2):
            left_at[(stop * 2 + image) * stride] = ABSENT
            right_at[(stop * 2 + image) * stride] = ABSENT
            out_at[image * stride] = slots

    def tables(index, _):
        image = index // panel
        slot = lax.rem(index, panel)
        for stop in range(2):
            entry = (stop * 2 + image) * stride + 1 + slot
            left = (left_ref if stop == 0 else left_next_ref)[image, slot]
            safe = jnp.maximum(left, 0)
            owner, within = safe // per_left, lax.rem(safe, per_left)
            if stop == 0:
                bucket = owner ^ col
                spot = (within // half) * (cols * half) + bucket * half + lax.rem(within, half)
                out_at[image * stride + 1 + slot] = jnp.where(left >= 0, spot, slots)
            else:
                after = lax.rem(col + 1, cols)
                bucket = owner ^ after
                crossing = lax.rem(after, middle) == 0
                turned = jnp.where(bucket < quarter, bucket, bucket + middle)
                turned = jnp.where(bucket < middle, turned, quarter + (owner ^ col))
                bucket = jnp.where(crossing, turned, bucket)
            late = bucket >= 3 * quarter
            early_at = (1 + (stop * 3 * quarter + bucket) * per_left + within) * SHIFT
            late_at = (1 + (stop * quarter + bucket - 3 * quarter) * per_left + within) * SHIFT + (1 << LATE)
            left_at[entry] = jnp.where(left >= 0, jnp.where(late, late_at, early_at), ABSENT)
            target = lax.rem(row + stop, rows)
            turned = jnp.where(row == rows - 1, 1 - image, image) if stop == 1 else image
            place = table_ref[target ^ row, rows * per_right + turned * panel + slot]
            safe = jnp.maximum(place, 0)
            source = (safe // per_right) ^ row
            block = table_ref[source, target * per_right + lax.rem(safe, per_right)]
            there = (place >= 0) & (block >= 0)
            rank = jnp.int32(0)
            for position, mask in enumerate(right_order(rows)):
                rank = jnp.where(source == mask, position, rank)
            relay = (rank >= rows.bit_length()).astype(jnp.int32) << RELAY
            right_at[entry] = jnp.where(there, stop * 2 * panel + index + relay, ABSENT)
            block_ref[stop * 2 * panel + index] = jnp.where(there, rank * own + block, 0)
        return 0

    lax.fori_loop(0, 2 * panel, tables, 0, unroll=2)

    def clear(index, _):
        count_ref[index] = 0
        return 0

    lax.fori_loop(0, 3 * slots + 8, clear, 0, unroll=8)
    total = jnp.int32(0)
    for stop in range(2):
        for image in range(2):
            base = (stop * 2 + image) * stride

            def read(step, found):
                codes, spots = [], []
                for lane in range(READ):
                    packed = triple_ref[(image * 2 + stop) * pairs + step * READ + lane]
                    codes.append(left_at[base + (packed & 255)] + right_at[base + ((packed >> 8) & 255)])
                    spots.append(out_at[image * stride + (packed >> 16)])
                for code, spot in zip(codes, spots):
                    live = (code >= 0) & (spot < slots)
                    chapter = (code >> RELAY) & 1 if stop == 0 else 1
                    chapter = jnp.where(((code >> LATE) & 1) == 1, 2, chapter)
                    key = jnp.where(live, spot + chapter * slots, 3 * slots)
                    raw_code[found] = (code & ((1 << LATE) - 1)) + (spot << LATE)
                    raw_key[found] = key
                    count_ref[key] = count_ref[key] + 1
                    found = found + live.astype(jnp.int32)
                return found

            total = lax.fori_loop(0, pairs // READ, read, total)

    def fill(index, _):
        code_ref[index] = slots << LATE
        return 0

    lax.fori_loop(0, code_ref.shape[0], fill, 0, unroll=16)

    def prefix(key, start):
        count = count_ref[key]
        count_ref[key] = start
        return start + (count + GROUP - 1) // GROUP * GROUP

    done = jnp.int32(0)
    bound_ref[0] = 0
    cuts = (0, slots, 2 * slots, 2 * slots + slots // 2, 3 * slots)
    for part, (low, high) in enumerate(zip(cuts[:-1], cuts[1:])):
        done = lax.fori_loop(low, high, prefix, done, unroll=8)
        done = (done + GROUP * UNROLL - 1) // (GROUP * UNROLL) * (GROUP * UNROLL)
        bound_ref[part + 1] = done // (GROUP * UNROLL)

    def place(index, _):
        key = raw_key[index]
        spot = count_ref[key]
        code_ref[spot] = raw_code[index]
        count_ref[key] = spot + 1
        return 0

    lax.fori_loop(0, total, place, 0)


def make_plan(place, triples, left_place, left_next, table, sizes):
    _, cols, _, per_left, _, panel, pairs = sizes
    slots = cols * per_left
    room = 4 * pairs + 3 * slots * (GROUP - 1) + 4 * GROUP * UNROLL
    room = (room + 127) // 128 * 128
    return pl.pallas_call(
        functools.partial(plan_body, sizes),
        out_shape=(
            jax.ShapeDtypeStruct((room,), jnp.int32),
            jax.ShapeDtypeStruct((5,), jnp.int32),
            jax.ShapeDtypeStruct((4 * panel,), jnp.int32),
        ),
        in_specs=[SMEM] * 5,
        out_specs=(SMEM,) * 3,
        scratch_shapes=[
            pltpu.SMEM((4 * (panel + 1),), jnp.int32),
            pltpu.SMEM((4 * (panel + 1),), jnp.int32),
            pltpu.SMEM((2 * (panel + 1),), jnp.int32),
            pltpu.SMEM((4 * pairs + 8,), jnp.int32),
            pltpu.SMEM((4 * pairs + 8,), jnp.int32),
            pltpu.SMEM((3 * slots + 8,), jnp.int32),
        ],
        cost_estimate=pl.CostEstimate(flops=40_000_000, bytes_accessed=60_000_000, transcendentals=0),
        name="plan",
    )(place, triples, left_place, left_next, table)


def halves(value):
    high = value.astype(jnp.bfloat16)
    return high, (value - high.astype(jnp.float32)).astype(jnp.bfloat16)


def take_body(masks, place_ref, list_ref, blocks_ref, *refs):
    outs, (held, in_sems, out_sems) = refs[: len(masks)], refs[len(masks) :]
    col = place_ref[1]
    cols, per_left = list_ref.shape
    for bucket, mask in enumerate(masks):
        peer = jnp.where(col < cols // 2, cols // 2, 0) if mask is None else col ^ mask
        for within in range(per_left):
            block = jnp.maximum(list_ref[peer, within], 0)
            pltpu.make_async_copy(blocks_ref.at[block], held.at[bucket, within], in_sems.at[bucket]).start()
    stores = []
    for bucket in range(len(masks)):
        pltpu.make_async_copy(held.at[bucket], held.at[bucket], in_sems.at[bucket]).wait()
        stores.append(pltpu.make_async_copy(held.at[bucket], outs[bucket], out_sems.at[bucket]))
        stores[-1].start()
    for store in stores:
        store.wait()


def take(masks, place, left_list, left_own):
    per_left, size = left_list.shape[1], left_own.shape[-1]
    return pl.pallas_call(
        functools.partial(take_body, masks),
        out_shape=[jax.ShapeDtypeStruct((per_left, size, size), jnp.float32)] * len(masks),
        in_specs=[SMEM] * 2 + [HBM],
        out_specs=[HBM] * len(masks),
        scratch_shapes=[
            pltpu.VMEM((len(masks), per_left, size, size), jnp.float32),
            pltpu.SemaphoreType.DMA((len(masks),)),
            pltpu.SemaphoreType.DMA((len(masks),)),
        ],
        compiler_params=pltpu.CompilerParams(vmem_limit_bytes=62 * 1024 * 1024),
        name="take",
    )(place, left_list, left_own)


def part_body(starts, *refs):
    count = len(starts)
    sources, outs, (held, in_sems, out_sems) = refs[:count], refs[count : 2 * count], refs[2 * count :]
    fetches, stores = [], []
    for index, start in enumerate(starts):
        length = outs[index].shape[0]
        target = held.at[index, pl.ds(0, length)]
        fetches.append(pltpu.make_async_copy(sources[index].at[pl.ds(start, length)], target, in_sems.at[index]))
        stores.append(pltpu.make_async_copy(target, outs[index], out_sems.at[index]))
    for fetch in fetches:
        fetch.start()
    for fetch, store in zip(fetches, stores):
        fetch.wait()
        store.start()
    for store in stores:
        store.wait()


def parted(wanted):
    size = wanted[0][0].shape[-1]
    longest = max(stop - start for _, start, stop in wanted)
    return pl.pallas_call(
        functools.partial(part_body, [start for _, start, _ in wanted]),
        out_shape=[jax.ShapeDtypeStruct((stop - start, size, size), jnp.float32) for _, start, stop in wanted],
        in_specs=[HBM] * len(wanted),
        out_specs=[HBM] * len(wanted),
        scratch_shapes=[
            pltpu.VMEM((len(wanted), longest, size, size), jnp.float32),
            pltpu.SemaphoreType.DMA((len(wanted),)),
            pltpu.SemaphoreType.DMA((len(wanted),)),
        ],
        compiler_params=pltpu.CompilerParams(vmem_limit_bytes=62 * 1024 * 1024),
        name="parted",
    )(*[array for array, _, _ in wanted])


DEPTH = 8
CHUNK = 8


def split_body(bases, *refs):
    sources, (out_ref, raw, cut, in_sems, out_sems) = refs[: len(bases)], refs[-5:]
    size = raw.shape[-1]
    steps = []
    for source, base in zip(sources, bases):
        for start in range(0, source.shape[0], CHUNK):
            steps.append((source, start, min(CHUNK, source.shape[0] - start), base + start))

    def fetch(step):
        source, start, count, _ = steps[step]
        slot = step % DEPTH
        return pltpu.make_async_copy(source.at[pl.ds(start, count)], raw.at[slot, pl.ds(0, count)], in_sems.at[slot])

    def store(step):
        _, _, count, base = steps[step]
        slot = step % DEPTH
        return pltpu.make_async_copy(cut.at[slot, pl.ds(0, count)], out_ref.at[pl.ds(base, count)], out_sems.at[slot])

    for step in range(min(DEPTH, len(steps))):
        fetch(step).start()
    for step in range(len(steps)):
        slot = step % DEPTH
        fetch(step).wait()
        if step >= DEPTH:
            store(step - DEPTH).wait()

        def convert(index, _):
            high, low = halves(raw[slot, index])
            cut[slot, index, :, 0:size] = high
            cut[slot, index, :, size : 2 * size] = low
            return 0

        lax.fori_loop(0, steps[step][2], convert, 0)
        store(step).start()
        if step + DEPTH < len(steps):
            fetch(step + DEPTH).start()
    for step in range(max(0, len(steps) - DEPTH), len(steps)):
        store(step).wait()


def split(pieces, count):
    size = pieces[0][0].shape[-1]
    return pl.pallas_call(
        functools.partial(split_body, [base for _, base in pieces]),
        out_shape=jax.ShapeDtypeStruct((count, size, 2 * size), jnp.bfloat16),
        in_specs=[HBM] * len(pieces),
        out_specs=HBM,
        scratch_shapes=[
            pltpu.VMEM((DEPTH, CHUNK, size, size), jnp.float32),
            pltpu.VMEM((DEPTH, CHUNK, size, 2 * size), jnp.bfloat16),
            pltpu.SemaphoreType.DMA((DEPTH,)),
            pltpu.SemaphoreType.DMA((DEPTH,)),
        ],
        cost_estimate=pl.CostEstimate(flops=0, bytes_accessed=2 * count * size * size * 4, transcendentals=0),
        name="split",
    )(*[piece for piece, _ in pieces])


def multiply_body(mode, part, kinds, sizes, place_ref, code_ref, bound_ref, block_ref, right_ref, *refs):
    _, cols, _, per_left, _, _, _ = sizes
    slots = cols * per_left
    half = per_left // 2
    relay_ref, refs = (refs[0], refs[1:]) if mode > 0 else (None, refs)
    direct = right_ref.shape[0]
    late, added = mode == 2, mode > 0
    spots = slots // 2 if late else slots
    outs = cols if late else 1
    count = len(kinds) + sum(kinds)
    sources, before_ref, rest = refs[:count], refs[count] if added else None, refs[count + added :]
    out_refs, (lefts, rights, total, raw, left_sems, right_sem, total_sem, out_sem) = rest[:outs], rest[outs:]
    size = raw.shape[-1]
    first = part * spots
    crossing = lax.rem(place_ref[1] + 1, cols // 2) == 0

    def fetch(source, bucket):
        return pltpu.make_async_copy(source, raw.at[pl.ds(bucket * per_left, per_left)], left_sems.at[bucket])

    def gather(index, _):
        block = block_ref[index]

        @pl.when(block < direct)
        def _():
            pltpu.make_async_copy(right_ref.at[block], rights.at[index], right_sem).start()

        @pl.when(block >= direct)
        def _():
            source = right_ref.at[0] if relay_ref is None else relay_ref.at[block - direct]
            pltpu.make_async_copy(source, rights.at[index], right_sem).start()

        return 0

    offset = 0
    for bucket, two in enumerate(kinds):
        if two:

            @pl.when(jnp.logical_not(crossing))
            def _():
                fetch(sources[offset], bucket).start()

            @pl.when(crossing)
            def _():
                fetch(sources[offset + 1], bucket).start()

        else:
            fetch(sources[offset], bucket).start()
        offset += 1 + two
    lax.fori_loop(0, rights.shape[0], gather, 0, unroll=4)
    if added:
        carried = pltpu.make_async_copy(before_ref.at[pl.ds(first, spots)], total.at[pl.ds(0, spots)], total_sem)
        carried.start()
        total[spots] = jnp.zeros(total.shape[1:], total.dtype)
    else:
        total[...] = jnp.zeros_like(total)
    lefts[0] = jnp.zeros(lefts.shape[1:], lefts.dtype)
    for bucket in range(len(kinds)):
        fetch(sources[0], bucket).wait()

        def convert(index, _):
            high, low = halves(raw[index])
            lefts[1 + index, :, 0:size] = high
            lefts[1 + index, :, size : 2 * size] = low
            return 0

        lax.fori_loop(bucket * per_left, (bucket + 1) * per_left, convert, 0, unroll=2)
    pltpu.make_async_copy(rights, rights, right_sem).wait()
    if added:
        carried.wait()

    def multiply(step, _):
        made = []
        for lane in range(UNROLL):
            start = (step * UNROLL + lane) * GROUP
            codes = [code_ref[start + index] for index in range(GROUP)]
            parts_left, parts_right = [], []
            for code in codes:
                parts_left.append(lefts[(code & ((1 << LATE) - 1)) // SHIFT])
                block = rights[code & (SHIFT - 1)]
                parts_right += [block, block]
            product = jnp.dot(
                jnp.concatenate(parts_left, axis=1),
                jnp.concatenate(parts_right, axis=0),
                preferred_element_type=jnp.float32,
            )
            made.append((jnp.minimum((codes[0] >> LATE) - first, spots), product))
        for spot, product in made:
            total[spot] += product[:, 0:size] + product[:, size : 2 * size]
        return 0

    chapter = mode + part
    lax.fori_loop(bound_ref[chapter], bound_ref[chapter + 1], multiply, 0)
    copies = []
    if late:
        for bucket in range(cols):
            copies.append(
                pltpu.make_async_copy(total.at[pl.ds(bucket * half, half)], out_refs[bucket], out_sem.at[bucket])
            )
    else:
        copies.append(pltpu.make_async_copy(total.at[pl.ds(0, slots)], out_refs[0], out_sem.at[0]))
    for entry in copies:
        entry.start()
    for entry in copies:
        entry.wait()


def multiplied(mode, part, sizes, place, plan, rights, lefts, before=None):
    _, cols, _, per_left, _, panel, _ = sizes
    slots = cols * per_left
    late = mode == 2
    spots = slots // 2 if late else slots
    size = rights[0].shape[1]
    rights = rights[: 1 + (mode > 0)]
    if late:
        out_shape = [jax.ShapeDtypeStruct((per_left // 2, size, size), jnp.float32)] * cols
        out_specs = [HBM] * cols
    else:
        out_shape, out_specs = jax.ShapeDtypeStruct((slots, size, size), jnp.float32), HBM
    arrays = [array for entry in lefts for array in entry] + ([before] if mode > 0 else [])
    return pl.pallas_call(
        functools.partial(multiply_body, mode, part, [len(entry) - 1 for entry in lefts], sizes),
        out_shape=out_shape,
        in_specs=[SMEM] * 4 + [HBM] * (len(rights) + len(arrays)),
        out_specs=out_specs,
        scratch_shapes=[
            pltpu.VMEM((len(lefts) * per_left + 1, size, 2 * size), jnp.bfloat16),
            pltpu.VMEM(((4 if mode > 0 else 2) * panel, size, 2 * size), jnp.bfloat16),
            pltpu.VMEM((spots + 1, size, size), jnp.float32),
            pltpu.VMEM((len(lefts) * per_left, size, size), jnp.float32),
            pltpu.SemaphoreType.DMA((len(lefts),)),
            pltpu.SemaphoreType.DMA,
            pltpu.SemaphoreType.DMA,
            pltpu.SemaphoreType.DMA((cols,)),
        ],
        cost_estimate=pl.CostEstimate(flops=0, bytes_accessed=4 * slots * size * size * 4, transcendentals=0),
        compiler_params=pltpu.CompilerParams(vmem_limit_bytes=(48 if late else 62) * 1024 * 1024),
    )(place, *plan, *rights, *arrays)


def collect_body(part, sizes, place_ref, list_ref, *refs):
    _, cols, _, per_left, _, _, _ = sizes
    half = per_left // 2
    sources, (out_ref, held, in_sems, out_sems) = refs[:cols], refs[-4:]
    slots = [(bucket, within) for bucket in range(cols) for within in range(half)]

    def each(action):
        for index, (bucket, within) in enumerate(slots):
            block = list_ref[place_ref[1] ^ bucket, part * half + within]

            @pl.when(block >= 0)
            def _():
                action(
                    pltpu.make_async_copy(sources[bucket].at[within], held.at[index], in_sems.at[index]),
                    pltpu.make_async_copy(held.at[index], out_ref.at[block], out_sems.at[index]),
                )

    def forward(fetch, store):
        fetch.wait()
        store.start()

    each(lambda fetch, store: fetch.start())
    each(forward)
    each(lambda fetch, store: store.wait())


def collected(part, sizes, place, left_list, backs, before):
    _, cols, own, per_left, _, _, _ = sizes
    size = backs[0].shape[-1]
    slots = cols * per_left // 2
    held = [] if before is None else [before]
    return pl.pallas_call(
        functools.partial(collect_body, part, sizes),
        out_shape=jax.ShapeDtypeStruct((own, size, size), jnp.float32),
        in_specs=[SMEM] * 2 + [HBM] * (len(backs) + len(held)),
        out_specs=HBM,
        input_output_aliases={2 + len(backs): 0} if held else {},
        scratch_shapes=[
            pltpu.VMEM((slots, size, size), jnp.float32),
            pltpu.SemaphoreType.DMA((slots,)),
            pltpu.SemaphoreType.DMA((slots,)),
        ],
    )(place, left_list, *backs, *held)


def send_order(cols):
    middle = cols // 2
    order = []
    for index in range(max(middle - 2, cols // 4)):
        order += [mask for mask in (2 + index, middle + index) if mask < (middle if mask < middle else 3 * cols // 4)]
    order = list(dict.fromkeys(order))
    return order + [mask for mask in range(1, cols) if mask not in order and mask > 1] + [1]


def local(left_blocks, right_blocks, left_send, left_place, right_send, right_place, triples):
    rows, cols = lax.axis_size("row"), lax.axis_size("col")
    row, col = lax.axis_index("row").astype(jnp.int32), lax.axis_index("col").astype(jnp.int32)
    place = jnp.stack([row, col])
    left_own, right_own = left_blocks[0, 0], right_blocks[0, 0]
    own = left_own.shape[0]
    left_list, right_list = left_send[0, 0], right_send[0, 0]
    positions = left_place[0, 0]
    per_left, per_right = left_list.shape[1], right_list.shape[1]
    panel, pairs = positions.shape[1], triples.shape[-1]
    sizes = (rows, cols, own, per_left, per_right, panel, pairs)
    middle, quarter = cols // 2, cols // 4
    back_one = lambda source: (source - 1) % cols

    masks = [1 << bit for bit in range((rows - 1).bit_length())]
    table_own = jnp.concatenate([right_list.reshape(-1), right_place[0, 0].reshape(-1)])
    tables = spread(table_own, "row", masks)
    table = jnp.stack([tables[mask] for mask in range(rows)])
    left_next = moved(positions, "col", back_one)

    cut = own // 2
    whole, low, high = {0: right_own}, {}, {}
    for mask in masks:
        whole[mask] = moved(right_own, "row", lambda source: source ^ mask)
    relays = [(key, 1 << (key.bit_length() - 1), key & -key) for key in right_order(rows)[len(whole) :]]
    lows = sorted({key ^ top for key, top, _ in relays} & set(masks))
    highs = sorted({key ^ bottom for key, _, bottom in relays} & set(masks))
    parts = parted([(whole[mask], 0, cut) for mask in lows] + [(whole[mask], cut, own) for mask in highs])
    low.update(zip(lows, parts[: len(lows)]))
    high.update(zip(highs, parts[len(lows) :]))
    for key, top, bottom in relays:
        low[key] = moved(low[key ^ top], "row", lambda source: source ^ top)
        high[key] = moved(high[key ^ bottom], "row", lambda source: source ^ bottom)

    order = send_order(cols)
    taken = list(take(order[:2], place, left_list, left_own))
    taken += list(take(order[2:] + [0, None], place, left_list, left_own))
    here = {}
    for index, mask in enumerate(order):
        here[mask] = moved(taken[index], "col", lambda source: source ^ mask)
    here[0], extra = taken[-2], {0: taken[-1]}
    for mask in range(1, middle):
        extra[mask] = moved(
            extra[0], "col", lambda source: source ^ mask, [(middle - 1) ^ mask, (cols - 1) ^ mask]
        )
    there = {}
    for mask in range(cols):
        among = None if mask < middle else [source for source in range(cols) if source % middle != 0]
        there[mask] = moved(here[mask], "col", back_one, among)

    shifted = triples[0, 0] + 1
    packed = (shifted[:, :, 0] + shifted[:, :, 1] * 256 + shifted[:, :, 2] * 65536).reshape(-1)
    plan = make_plan(place, packed, positions, left_next, table, sizes)
    direct = split([(whole[mask], index * own) for index, mask in enumerate(whole)], len(whole) * own)
    pieces = []
    for index, mask in enumerate(right_order(rows)[len(whole) :]):
        pieces += [(low[mask], index * own), (high[mask], index * own + cut)]
    relayed = split(pieces, (rows - len(whole)) * own)
    rights = (direct, relayed)
    first = [(here[mask],) for mask in range(3 * quarter)]
    second = first + [(there[mask],) for mask in range(quarter)]
    second += [(there[mask], extra[mask - quarter]) for mask in range(quarter, 3 * quarter)]
    late = [(here[mask],) for mask in range(3 * quarter, cols)]
    late += [(there[mask], there[mask - middle]) for mask in range(3 * quarter, cols)]
    before = multiplied(0, 0, sizes, place, plan, rights, first)
    before = multiplied(1, 0, sizes, place, plan, rights, second, before)
    result = None
    backs = []
    for part in range(2):
        product = multiplied(2, part, sizes, place, plan, rights, late, before)
        returned = {0: product[0]}
        for mask in list(range(middle, cols)) + list(range(1, middle)):
            returned[mask] = moved(product[mask], "col", lambda source: source ^ mask)
        backs.append([returned[mask] for mask in range(cols)])
    for part in range(2):
        result = collected(part, sizes, place, left_list, backs[part], result)
    return result[None, None]


def solution(mesh):
    placed = (
        P("row", "col", None, None, None),
        P("row", "col", None, None, None),
        P("row", "col", None, None),
        P("row", "col", None, None),
        P("row", "col", None, None),
        P("row", "col", None, None),
        P("row", "col", None, None, None, None),
    )

    return jax.shard_map(
        local,
        mesh=mesh,
        in_specs=placed,
        out_specs=P("row", "col", None, None, None),
        check_vma=False,
    )
```
